32 devices in a mesh: paths: 4 (over y, core), factors: 8 (over z, x).
Axes of the slice: x: 2, y: 2, z: 4, core: 2. Of those that a mesh axis runs over, the one named last changes fastest.
Arguments:
- x_start: float32 [512, 2048], P('factors', 'paths'), may hold values from -3 to 3
- shocks: float32 [4, 512, 2048], P(None, 'factors', 'paths'), may hold values from -6 to 6
- cholesky: float32 [512, 512], P(None, 'factors'), as said below
- reversion: float32 [512], P('factors'), may hold values from 0.05 to 2
- sabr_alpha: float32 [64], replicated, may hold values from 0.2 to 0.6
- sabr_rho: float32 [64], replicated, may hold values from -0.7 to 0.7
- sabr_nu: float32 [64], replicated, may hold values from 0.3 to 1.5
- factor_slice: int32 [512], P('factors'), may hold values from 0 to 63
- notional: float32 [32768], P('factors'), may hold values from -1 to 1
- strike: float32 [32768], P('factors'), may hold values from -3 to 3
- trade_set: int32 [32768], P('factors'), may hold values from 0 to 255
- trade_factor: int32 [32768], P('factors'), may hold values from 0 to 511, as said below
- loss_given: float32 [256], replicated, may hold values from 0.2 to 0.8
Outputs:
- path_adjoint: float32 [512, 2048], P('factors', 'paths')
- sabr_grad: float32 [3, 64], replicated
The draws below stay inside these ranges and needn't reach their ends.
Inputs may be any that keep to these rules, and one draw needn't show every extreme that they name: `cholesky`: lower triangular with a positive diagonal and rows of unit length. `trade_factor`: trade t's factor lies in [(t // 4096) * 64, (t // 4096 + 1) * 64).
All inputs are finite; a program needn't handle non-finite values.
Results may differ from the reference program's by a relative error of at most 0.004.
Values may be sent and summed in bfloat16 or wider, within the bound.
A program may use at most 192 MiB of HBM per device.

```python
import math
import jax
import jax.numpy as jnp
import numpy as np
from jax import lax

F = 512
SLICES = 64
STEPS = 4
P_DEV = 512
TRADES_DEV = 4096
F_DEV = 64
NPATHS = 2048
TRADES = 32768
NSETS = 256
N_PATHS = 4


def draw_cholesky(key, part):
    subkeys = jax.random.split(jax.random.fold_in(key, 11), 4)
    normal_draw = jax.random.normal(subkeys[0], (F, F), jnp.float32)
    row_index = jnp.arange(F)[:, None]
    col_index = jnp.arange(F)[None, :]
    strict_lower = jnp.where(col_index < row_index, normal_draw / jnp.sqrt(jnp.maximum(row_index, 1).astype(jnp.float32)), 0.0)
    row_loading = jax.random.uniform(subkeys[2], (F, 1), jnp.float32, 0.5, 1.5)
    col_sign = jnp.where(jax.random.uniform(subkeys[3], (1, F), jnp.float32) < 0.5, -1.0, 1.0)
    sector = jnp.where((col_index < row_index) & (col_index < F_DEV), 0.8 * row_loading * col_sign / jnp.sqrt(jnp.float32(F_DEV)), 0.0)
    diagonal = jax.random.uniform(subkeys[1], (F,), jnp.float32, 0.5, 1.5)
    triangle = strict_lower + sector + jnp.diag(diagonal)
    return triangle / jnp.sqrt(jnp.sum(triangle * triangle, axis=1, keepdims=True))


def draw_trade_factor(key, part):
    position = jnp.arange(TRADES, dtype=jnp.int32)
    within = position % TRADES_DEV
    offset = jax.random.randint(jax.random.fold_in(key, 23), (TRADES,), 0, F_DEV, dtype=jnp.int32)
    offset = jnp.where(within == 0, 0, jnp.where(within == TRADES_DEV - 1, F_DEV - 1, offset))
    return (position // TRADES_DEV * F_DEV + offset).astype(jnp.int32)


def touch_ends(result, own_key, low, top_value):
    spot = [jax.random.randint(jax.random.fold_in(own_key, axis), (), 0, length) for axis, length in enumerate(result.shape)]
    widest = result.shape.index(max(result.shape))
    beside = spot[:widest] + [(spot[widest] + 1) % result.shape[widest]] + spot[widest + 1:]
    return result.at[tuple(spot)].set(low).at[tuple(beside)].set(top_value)


def steps_of(own_key, shape, shards, smallest, high):
    loudness, own = 1.0, jax.random.fold_in(own_key, 6)
    for axis_at, blocks in shards:
        steps = jnp.exp(jax.random.uniform(jax.random.fold_in(own, axis_at), (blocks,), jnp.float32, smallest / len(shards), high / len(shards)))
        loudness = loudness * jnp.repeat(steps, shape[axis_at] // blocks).reshape([-1 if axis == axis_at else 1 for axis in range(len(shape))])
    return loudness


def rank_bounds(amount, slope):
    loads = [(1 << 20) // math.isqrt(grade ** slope) + 1 for grade in range(1, amount + 1)]
    width = 1 + sum(loads) // (1 << 30)
    return np.cumsum(np.array([max(1, weight // width) for weight in loads]))


def ranked_ids(key, extent, number_of, slope):
    listing = rank_bounds(number_of, slope)
    pick = jax.random.randint(jax.random.fold_in(key, 1), extent, 0, int(listing[number_of - 1]))
    standing = jnp.searchsorted(jnp.asarray(listing, jnp.int32), pick, side="right")
    return jax.random.permutation(jax.random.fold_in(key, 2), number_of)[standing].astype(jnp.int32)


def centred(stream_key, dims, scale, limit, shards=(), kind=jnp.bfloat16):
    result = jax.random.normal(stream_key, dims, jnp.float32) * scale
    if len(shards) > 0:
        result = steps_of(stream_key, dims, shards, -0.22, 0.18) * result
    return jnp.clip(result, min=-limit, max=limit).astype(kind)


def setup_inputs(seed: int = 0) -> dict:
    key_list = jax.random.split(jax.random.key(seed), 14)
    return {
        "x_start": centred(key_list[0], (F, NPATHS), 0.5, 3.0, ((0, 8), (1, 4)), jnp.float32),
        "shocks": centred(key_list[1], (STEPS, F, NPATHS), 1.0, 6.0, ((1, 8), (2, 4)), jnp.float32),
        "cholesky": draw_cholesky(jax.random.fold_in(key_list[13], 71), 0),
        "reversion": jnp.clip(jnp.exp(math.log(2.0) - 3.6888794 * jax.random.uniform(key_list[3], (F,), jnp.float32) ** steps_of(key_list[3], (F,), ((0, 8),), -0.2, 0.2)), 0.05, 2.0),
        "sabr_alpha": jnp.clip(jax.random.uniform(key_list[4], (SLICES,), jnp.float32, 0.2, 0.6), 0.2, 0.6),
        "sabr_rho": jnp.clip(jax.random.uniform(key_list[5], (SLICES,), jnp.float32, -0.7, 0.7), -0.7, 0.7),
        "sabr_nu": jnp.clip(jnp.exp(jax.random.uniform(key_list[6], (SLICES,), jnp.float32, math.log(0.3), math.log(1.5))), 0.3, 1.5),
        "factor_slice": touch_ends(jax.random.randint(key_list[7], (F,), 0, SLICES), jax.random.fold_in(key_list[7], 1), 0, SLICES - 1).astype(jnp.int32),
        "notional": centred(key_list[8], (TRADES,), 0.15, 1.0, ((0, 8),), jnp.float32),
        "strike": centred(key_list[9], (TRADES,), 0.5, 3.0, ((0, 8),), jnp.float32),
        "trade_set": touch_ends(ranked_ids(key_list[10], (TRADES,), NSETS, 2), jax.random.fold_in(key_list[10], 3), 0, NSETS - 1).astype(jnp.int32),
        "trade_factor": draw_trade_factor(jax.random.fold_in(key_list[13], 71), 0),
        "loss_given": jnp.clip(jax.random.uniform(key_list[12], (NSETS,), jnp.float32, 0.2, 0.8), 0.2, 0.8),
    }


TIME_STEP = 0.25
ROOT_STEP = 0.5
DISCOUNT_RATE = 0.03
PRECISE = lax.Precision.HIGHEST


def smile_terms(squashed, alpha_rows, rho_rows, nu_rows):
    curve = (2.0 - 3.0 * rho_rows * rho_rows) * nu_rows * nu_rows / 24.0
    base = 1.0 + 0.5 * rho_rows * nu_rows * squashed + curve * squashed * squashed
    rho_slope = alpha_rows * (0.5 * nu_rows * squashed - 0.25 * rho_rows * nu_rows * nu_rows * squashed * squashed)
    nu_slope = alpha_rows * (0.5 * rho_rows * squashed + (2.0 - 3.0 * rho_rows * rho_rows) * nu_rows * squashed * squashed / 12.0)
    level_slope = alpha_rows * (0.5 * rho_rows * nu_rows + 2.0 * curve * squashed)
    return alpha_rows * base, base, rho_slope, nu_slope, level_slope


def reference(x_start, shocks, cholesky, reversion, sabr_alpha, sabr_rho, sabr_nu, factor_slice, notional, strike, trade_set, trade_factor, loss_given):
    alpha_rows = sabr_alpha[factor_slice][:, None]
    rho_rows = sabr_rho[factor_slice][:, None]
    nu_rows = sabr_nu[factor_slice][:, None]
    damping = (1.0 - reversion * TIME_STEP)[:, None]
    blocks = N_PATHS
    block_width = P_DEV
    starts = x_start.reshape(F, blocks, block_width).transpose(1, 0, 2)
    shock_blocks = shocks.reshape(STEPS, F, blocks, block_width).transpose(2, 0, 1, 3)

    def run_block(block_pair):
        state, shock_block = block_pair
        states = [state]
        weights = []
        for step_index in range(STEPS):
            squashed = jnp.tanh(state)
            local_vol = smile_terms(squashed, alpha_rows, rho_rows, nu_rows)[0]
            mixed = jnp.dot(cholesky, local_vol * shock_block[step_index], precision=PRECISE)
            state = damping * state + ROOT_STEP * mixed
            states.append(state)
            moneyness = jnp.take(state, trade_factor, axis=0) - strike[:, None]
            values = (notional[:, None] * jnp.tanh(moneyness)).astype(jnp.bfloat16)
            exposure = jax.ops.segment_sum(values.astype(jnp.float32), trade_set, num_segments=NSETS)
            discount = math.exp(-DISCOUNT_RATE * TIME_STEP * (step_index + 1))
            weights.append((discount * loss_given[:, None] * jax.nn.sigmoid(exposure)).astype(jnp.bfloat16))
        adjoint = jnp.zeros_like(state)
        factor_sums = jnp.zeros((3, F), jnp.float32)
        for step_index in reversed(range(STEPS)):
            moneyness = jnp.take(states[step_index + 1], trade_factor, axis=0) - strike[:, None]
            squash_trade = jnp.tanh(moneyness)
            trade_adjoint = jnp.take(weights[step_index].astype(jnp.float32), trade_set, axis=0)
            trade_term = notional[:, None] * (1.0 - squash_trade * squash_trade) * trade_adjoint
            adjoint = adjoint + jax.ops.segment_sum(trade_term, trade_factor, num_segments=F)
            shock_adjoint = jnp.dot(cholesky.T, ROOT_STEP * adjoint, precision=PRECISE)
            squashed = jnp.tanh(states[step_index])
            local_vol, base, rho_slope, nu_slope, level_slope = smile_terms(squashed, alpha_rows, rho_rows, nu_rows)
            vol_adjoint = shock_adjoint * shock_block[step_index]
            factor_sums = factor_sums + jnp.stack([jnp.sum(vol_adjoint * base, axis=1), jnp.sum(vol_adjoint * rho_slope, axis=1), jnp.sum(vol_adjoint * nu_slope, axis=1)])
            adjoint = damping * adjoint + vol_adjoint * level_slope * (1.0 - squashed * squashed)
        return adjoint, factor_sums

    adjoints, sums = lax.map(run_block, (starts, shock_blocks))
    path_adjoint = adjoints.transpose(1, 0, 2).reshape(F, blocks * block_width)
    factor_sums = jnp.sum(sums, axis=0)
    sabr_grad = jax.ops.segment_sum(factor_sums.T, factor_slice, num_segments=SLICES).T / (blocks * block_width)
    return path_adjoint, sabr_grad
```

```python
import functools
import math

import jax
import jax.numpy as jnp
from jax import lax
from jax.experimental import pallas as pl
from jax.experimental.pallas import tpu as pltpu
from jax.sharding import PartitionSpec as P

TIME_STEP = 0.25
ROOT_STEP = 0.5
DISCOUNT_RATE = 0.03
PRECISE = lax.Precision.HIGHEST
MESH = pl.DeviceIdType.MESH
NN = (((1,), (0,)), ((), ()))
NT = (((1,), (1,)), ((), ()))
F32 = jnp.float32
BF16 = jnp.bfloat16
SHARES = 2
INNER = 2
PAD = 16
LANES = 128
UNROLL = 4


def mm(a, b, dims):
    return lax.dot_general(a, b, dims, preferred_element_type=F32)


def split(a):
    high = a.astype(BF16)
    return high, (a - high.astype(F32)).astype(BF16)


def split_mm(a, b, dims):
    rows = a.shape[0]
    both = mm(jnp.concatenate(split(a), axis=0), b, dims)
    return both[:rows] + both[rows:]


def one_hot(ids, count, value=None):
    shape = (count, ids.shape[1])
    rows = lax.broadcasted_iota(jnp.int16, shape, 0)
    value = jnp.ones((1, 1), BF16) if value is None else value.astype(BF16)
    hit = rows == jnp.broadcast_to(ids.astype(jnp.int16), shape)
    return jnp.where(hit, jnp.broadcast_to(value, shape), jnp.zeros(shape, BF16))


def fused_kernel(
    x_ref,
    shocks_ref,
    lt_ref,
    reversion_ref,
    smile_ref,
    slice_ref,
    notional_ref,
    strike_ref,
    set_ref,
    factor_ref,
    loss_ref,
    a_ref,
    g_ref,
    lt,
    par,
    xs_send,
    xs,
    trades,
    states,
    parts,
    squashes,
    exposure,
    weights,
    terms,
    back_send,
    back,
    grads,
    totals,
    line_send,
    line_recv,
    side_send,
    side_recv,
    twin_send,
    twin_recv,
    par_send,
    par_recv,
    path_send,
    path_recv,
    back_send_sem,
    back_recv_sem,
    grad_send,
    grad_recv,
    total_send,
    total_recv,
):
    steps, width, path_cols = shocks_ref.shape
    outer, inner = lt.shape[0], lt.shape[1]
    groups = outer * inner
    factors = lt.shape[3]
    paths = path_cols // groups
    path_groups = totals.shape[0]
    sets = loss_ref.shape[1]
    slices = smile_ref.shape[1]
    shares, tile = trades.shape[2], trades.shape[5]
    tiles = groups * shares
    rows = steps * paths
    bits = (sets - 1).bit_length()
    share_rows = width // shares

    me_f = lax.axis_index("factors")
    me_p = lax.axis_index("paths")
    me_o, me_i = me_f // inner, me_f % inner
    core = me_p % shares
    twin = me_p + 1 - 2 * core

    barrier = pltpu.get_barrier_semaphore()
    for d in range(1, groups):
        peer = {"factors": (me_f + d) % groups}
        pl.semaphore_signal(barrier, inc=1, device_id=peer, device_id_type=MESH)
    for d in range(1, path_groups):
        peer = {"paths": (me_p + d) % path_groups}
        pl.semaphore_signal(barrier, inc=1, device_id=peer, device_id_type=MESH)

    own_rows = pl.ds(pl.multiple_of(core * share_rows, share_rows), share_rows)
    lt[me_o, me_i, own_rows] = lt_ref[own_rows].astype(BF16)
    slice_rows = lax.broadcasted_iota(jnp.int32, (slices, width), 0)
    picked = jnp.where(slice_rows == slice_ref[...], 1.0, 0.0)
    smile = lax.dot_general(
        smile_ref[...], picked, NN, precision=PRECISE, preferred_element_type=F32
    )
    par[me_f] = jnp.concatenate(
        [smile[:3], reversion_ref[...], slice_ref[...].astype(F32), smile[:3]], axis=0
    )
    high = x_ref[...].astype(BF16).astype(F32)
    xs_send[0] = jnp.concatenate([high, x_ref[...] - high], axis=0).T.astype(BF16)
    for k in range(steps // 2):
        pair = jnp.concatenate([shocks_ref[2 * k], shocks_ref[2 * k + 1]], axis=0)
        xs_send[k + 1] = pair.T.astype(BF16)
    mine = pl.ds(pl.multiple_of(me_f * paths, paths), paths)
    for k in range(steps // 2 + 1):
        xs[me_f, k] = xs_send[k, mine, :]
    cols = pl.ds(pl.multiple_of(core * tile, tile), tile)
    code = set_ref[:, cols] + ((factor_ref[:, cols] - me_f * width) << bits)
    trades[me_o, me_i, core, 0] = notional_ref[:, cols]
    trades[me_o, me_i, core, 1] = strike_ref[:, cols]
    trades[me_o, me_i, core, 2] = code.astype(F32)

    pl.semaphore_wait(barrier, groups - 1 + path_groups - 1)

    def remote(ref, send, recv, peer):
        return pltpu.make_async_remote_copy(
            src_ref=ref, dst_ref=ref, send_sem=send, recv_sem=recv, device_id=peer, device_id_type=MESH
        )

    def block(kind, at_o, at_i, share):
        if kind == 0:
            share_at = pl.ds(pl.multiple_of(share * share_rows, share_rows), share_rows)
            return lt.at[at_o, at_i, share_at]
        return trades.at[at_o, at_i, share]

    every = pl.ds(0, outer)

    def line_copy(kind, d, at_o):
        return remote(
            block(kind, at_o, me_i, core),
            line_send.at[kind, d],
            line_recv.at[kind, d],
            {"factors": (me_o + d) % outer * inner + me_i},
        )

    def side_copy(kind, d, at_i):
        return remote(
            block(kind, every, at_i, core),
            side_send.at[kind, d],
            side_recv.at[kind, d],
            {"factors": me_o * inner + (me_i + d) % inner},
        )

    def twin_copy(kind, d, at_i, share):
        return remote(
            block(kind, every, at_i, share),
            twin_send.at[kind, d],
            twin_recv.at[kind, d],
            {"paths": twin},
        )

    def par_copy(d, at):
        return remote(par.at[at], par_send.at[d], par_recv.at[d], {"factors": (me_f + d) % groups})

    def path_copy(k, d, at):
        peer = (me_f + d) % groups
        theirs = pl.ds(pl.multiple_of(peer * paths, paths), paths)
        return pltpu.make_async_remote_copy(
            src_ref=xs_send.at[k, theirs],
            dst_ref=xs.at[at, k],
            send_sem=path_send.at[k, d],
            recv_sem=path_recv.at[k, d],
            device_id={"factors": peer},
            device_id_type=MESH,
        )

    sent = []

    def start(copy):
        copy.start()
        sent.append(copy)

    def start_line(kind):
        for d in range(1, outer):
            start(line_copy(kind, d, me_o))

    def line_to_side(kind):
        for d in range(1, outer):
            line_copy(kind, d, (me_o - d + outer) % outer).wait_recv()
        for d in range(1, inner):
            start(side_copy(kind, d, me_i))
        start(twin_copy(kind, 0, me_i, core))

    def side_to_twin(kind):
        for d in range(1, inner):
            at = (me_i - d + inner) % inner
            side_copy(kind, d, at).wait_recv()
            start(twin_copy(kind, d, at, core))

    def wait_twin(kind):
        for d in range(inner):
            twin_copy(kind, d, (me_i - d + inner) % inner, 1 - core).wait_recv()

    def wait_paths(k):
        for d in range(1, groups):
            path_copy(k, d, (me_f - d + groups) % groups).wait_recv()

    start_line(0)
    for d in range(1, groups):
        start(par_copy(d, me_f))
    for k in range(2):
        for d in range(1, groups):
            start(path_copy(k, d, me_f))
    start_line(1)
    for k in range(2, steps // 2 + 1):
        for d in range(1, groups):
            start(path_copy(k, d, me_f))

    line_to_side(0)
    line_to_side(1)
    for d in range(1, groups):
        par_copy(d, (me_f - d + groups) % groups).wait_recv()
    all_par = jnp.concatenate([par[g] for g in range(groups)], axis=1)
    alpha, rho, nu = all_par[0:1, :], all_par[1:2, :], all_par[2:3, :]
    damping = 1.0 - all_par[3:4, :] * TIME_STEP
    curve2 = 2.0 - 3.0 * rho * rho
    curve = curve2 * nu * nu / 24.0
    tilt = 0.5 * rho * nu

    def arrived(k):
        both = [xs[g, k].astype(F32) for g in range(groups)]
        return (
            jnp.concatenate([b[:, :width] for b in both], axis=1),
            jnp.concatenate([b[:, width:] for b in both], axis=1),
        )

    side_to_twin(0)
    wait_paths(0)
    state_parts = arrived(0)
    state = state_parts[0] + state_parts[1]
    wait_twin(0)
    corr = lt[...].reshape(factors, factors)
    shocks = []
    ones = jnp.ones((paths, PAD), BF16)
    for k in range(steps):
        if k % 2 == 0:
            wait_paths(k // 2 + 1)
            shocks.extend(arrived(k // 2 + 1))
        states[k] = state
        u = jnp.tanh(state)
        source = alpha * (1.0 + tilt * u + curve * u * u) * shocks[k]
        state = damping * state + ROOT_STEP * split_mm(source, corr, NN)
        high, low = split(state)
        for b in range(groups):
            cols = slice(b * width, (b + 1) * width)
            parts[b, k * paths : (k + 1) * paths, :] = jnp.concatenate(
                [high[:, cols], low[:, cols], ones], axis=1
            )
        if k == 0:
            side_to_twin(1)
    wait_twin(1)

    exposure[...] = jnp.zeros_like(exposure)

    def trade_rows(i):
        b, h = i // shares, i % shares
        at_o, at_i = b // inner, b % inner
        code = trades[at_o, at_i, h, 2].astype(jnp.int32)
        return b, trades[at_o, at_i, h, 0], trades[at_o, at_i, h, 1], code & ((1 << bits) - 1), code >> bits

    def forward(i, carry):
        b, notional, strike, in_set, factor = trade_rows(i)
        table = one_hot(factor, width)
        high, low = split(-strike)
        tail = jnp.concatenate([high, low, jnp.zeros((PAD - 2, tile), BF16)], axis=0)
        money = mm(parts[b], jnp.concatenate([table, table, tail], axis=0), NN)
        squash = jnp.tanh(money).astype(BF16)
        squashes[i] = squash
        exposure[...] += mm(squash, one_hot(in_set, sets, notional), NT)
        return carry

    lax.fori_loop(0, tiles, forward, 0, unroll=UNROLL)

    for k in range(steps):
        at = slice(k * paths, (k + 1) * paths)
        scale = math.exp(-DISCOUNT_RATE * TIME_STEP * (k + 1)) * loss_ref[...]
        weights[at, :] = (scale * jax.nn.sigmoid(exposure[at, :])).astype(BF16)
    terms[...] = jnp.zeros_like(terms)

    def backward(i, carry):
        b, notional, strike, in_set, factor = trade_rows(i)
        pulled = mm(weights[...], one_hot(in_set, sets, notional), NN)
        squash = squashes[i].astype(F32)
        pulled = (pulled * (1.0 - squash * squash)).astype(BF16)
        terms[b] += mm(pulled, one_hot(factor, width), NT)
        return carry

    lax.fori_loop(0, tiles, backward, 0, unroll=UNROLL)

    adjoint = jnp.zeros((paths, factors), F32)
    sums = [jnp.zeros((1, factors), F32) for _ in range(3)]
    for k in reversed(range(steps)):
        adjoint = adjoint + jnp.concatenate(
            [terms[b, k * paths : (k + 1) * paths, :] for b in range(groups)], axis=1
        )
        u = jnp.tanh(states[k])
        vbar = split_mm(ROOT_STEP * adjoint, corr, NT) * shocks[k]
        for at, slope in enumerate(
            (
                1.0 + tilt * u + curve * u * u,
                alpha * (0.5 * nu * u - 0.25 * rho * nu * nu * u * u),
                alpha * (0.5 * rho * u + curve2 * nu * u * u / 12.0),
            )
        ):
            sums[at] = sums[at] + jnp.sum(vbar * slope, axis=0, keepdims=True)
        adjoint = damping * adjoint + vbar * (alpha * (tilt + 2.0 * curve * u)) * (1.0 - u * u)

    folds = back.shape[2] // width
    depth = paths // folds
    for g in range(groups):
        cols = slice(g * width, (g + 1) * width)
        back_send[g] = jnp.concatenate(
            [adjoint[i * depth : (i + 1) * depth, cols] for i in range(folds)], axis=1
        )

    def back_copy(d, at):
        peer = (me_f + d) % groups
        return pltpu.make_async_remote_copy(
            src_ref=back_send.at[peer],
            dst_ref=back.at[at],
            send_sem=back_send_sem.at[d],
            recv_sem=back_recv_sem.at[d],
            device_id={"factors": peer},
            device_id_type=MESH,
        )

    def grad_copy(d, at):
        return remote(grads.at[at], grad_send.at[d], grad_recv.at[d], {"factors": (me_f + d) % groups})

    def total_copy(d, at):
        peer = {"paths": (me_p + d) % path_groups}
        return remote(totals.at[at], total_send.at[d], total_recv.at[d], peer)

    for d in range(1, groups):
        start(back_copy(d, me_f))
    back[me_f] = back_send[me_f]

    slice_rows = lax.broadcasted_iota(jnp.int32, (slices, factors), 0).astype(F32)
    slice_table = jnp.where(slice_rows == all_par[4:5, :], 1.0, 0.0)
    grads[me_f] = lax.dot_general(
        jnp.concatenate(sums + [jnp.zeros((5, factors), F32)], axis=0),
        slice_table,
        NT,
        precision=PRECISE,
        preferred_element_type=F32,
    )
    for d in range(1, groups):
        start(grad_copy(d, me_f))
    for d in range(1, groups):
        grad_copy(d, (me_f - d + groups) % groups).wait_recv()
    totals[me_p] = jnp.sum(grads[...], axis=0)
    for d in range(1, path_groups):
        start(total_copy(d, me_p))

    for d in range(1, groups):
        back_copy(d, (me_f - d + groups) % groups).wait_recv()
    pieces = []
    for g in range(groups):
        piece = back[g]
        pieces.extend(piece[:, i * width : (i + 1) * width] for i in range(folds))
    a_ref[...] = jnp.concatenate(pieces, axis=0).T

    for d in range(1, path_groups):
        total_copy(d, (me_p - d + path_groups) % path_groups).wait_recv()
    g_ref[...] = jnp.sum(totals[...], axis=0)[:3] / (path_cols * path_groups)
    for copy in sent:
        copy.wait_send()


def per_device(
    x_start,
    shocks,
    cholesky,
    reversion,
    sabr_alpha,
    sabr_rho,
    sabr_nu,
    factor_slice,
    notional,
    strike,
    trade_set,
    trade_factor,
    loss_given,
):
    width, path_cols = x_start.shape
    steps = shocks.shape[0]
    factors = cholesky.shape[0]
    groups = lax.axis_size("factors")
    path_groups = lax.axis_size("paths")
    outer, inner = groups // INNER, INNER
    paths = path_cols // groups
    tile = notional.shape[0] // SHARES
    tiles = groups * SHARES
    rows, sets, slices = steps * paths, loss_given.shape[0], sabr_alpha.shape[0]
    fold = LANES // width
    pairs = steps // 2 + 1
    smile = jnp.stack([sabr_alpha, sabr_rho, sabr_nu, sabr_alpha] * 2)
    vmem, dma = pltpu.VMEM, pltpu.SemaphoreType.DMA
    return pl.pallas_call(
        fused_kernel,
        out_shape=(
            jax.ShapeDtypeStruct((width, path_cols), F32),
            jax.ShapeDtypeStruct((3, slices), F32),
        ),
        in_specs=[pl.BlockSpec(memory_space=pltpu.VMEM)] * 11,
        out_specs=(pl.BlockSpec(memory_space=pltpu.VMEM),) * 2,
        scratch_shapes=[
            vmem((outer, inner, width, factors), BF16),
            vmem((groups, 8, width), F32),
            vmem((pairs, path_cols, 2 * width), BF16),
            vmem((groups, pairs, paths, 2 * width), BF16),
            vmem((outer, inner, SHARES, 3, 1, tile), F32),
            vmem((steps, paths, factors), F32),
            vmem((groups, rows, 2 * width + PAD), BF16),
            vmem((tiles, rows, tile), BF16),
            vmem((rows, sets), F32),
            vmem((rows, sets), BF16),
            vmem((groups, rows, width), F32),
            vmem((groups, paths // fold, LANES), F32),
            vmem((groups, paths // fold, LANES), F32),
            vmem((groups, 8, slices), F32),
            vmem((path_groups, 8, slices), F32),
            dma((2, outer)),
            dma((2, outer)),
            dma((2, inner)),
            dma((2, inner)),
            dma((2, inner)),
            dma((2, inner)),
            dma((groups,)),
            dma((groups,)),
            dma((pairs, groups)),
            dma((pairs, groups)),
            dma((groups,)),
            dma((groups,)),
            dma((groups,)),
            dma((groups,)),
            dma((path_groups,)),
            dma((path_groups,)),
        ],
        compiler_params=pltpu.CompilerParams(
            collective_id=0, has_side_effects=True, vmem_limit_bytes=56 * 1024 * 1024
        ),
    )(
        x_start,
        shocks,
        cholesky.T,
        reversion[None, :],
        smile,
        factor_slice[None, :],
        notional[None, :],
        strike[None, :],
        trade_set[None, :],
        trade_factor[None, :],
        loss_given[None, :],
    )


def solution(mesh):
    return jax.shard_map(
        per_device,
        mesh=mesh,
        in_specs=(
            P("factors", "paths"),
            P(None, "factors", "paths"),
            P(None, "factors"),
            P("factors"),
            P(),
            P(),
            P(),
            P("factors"),
            P("factors"),
            P("factors"),
            P("factors"),
            P("factors"),
            P(),
        ),
        out_specs=(P("factors", "paths"), P()),
        check_vma=False,
    )
```

```python
import functools
import math

import jax
import jax.numpy as jnp
from jax import lax
from jax.experimental import pallas as pl
from jax.experimental.pallas import tpu as pltpu
from jax.sharding import PartitionSpec as P

TIME_STEP = 0.25
ROOT_STEP = 0.5
DISCOUNT_RATE = 0.03
PRECISE = lax.Precision.HIGHEST
MESH = pl.DeviceIdType.MESH
NN = (((1,), (0,)), ((), ()))
NT = (((1,), (1,)), ((), ()))
F32 = jnp.float32
BF16 = jnp.bfloat16
SHARES = 4
PAD = 16
LANES = 128
UNROLL = 8


def mm(a, b, dims):
    return lax.dot_general(a, b, dims, preferred_element_type=F32)


def split(a):
    high = a.astype(BF16)
    return high, (a - high.astype(F32)).astype(BF16)


def split_mm(a, b, dims):
    rows = a.shape[0]
    both = mm(jnp.concatenate(split(a), axis=0), b, dims)
    return both[:rows] + both[rows:]


def one_hot(ids, count, value=None):
    shape = (count, ids.shape[1])
    rows = lax.broadcasted_iota(jnp.int16, shape, 0)
    value = jnp.ones((1, 1), BF16) if value is None else value.astype(BF16)
    hit = rows == jnp.broadcast_to(ids.astype(jnp.int16), shape)
    return jnp.where(hit, jnp.broadcast_to(value, shape), jnp.zeros(shape, BF16))


def pieces_before(g, per_chunk, chunks):
    level = g // per_chunk
    return per_chunk * (chunks * level - level * (level - 1) // 2) + g % per_chunk * (chunks - level)


def fused_kernel(
    x_hbm,
    shocks_hbm,
    lt_hbm,
    reversion_ref,
    alpha_ref,
    rho_ref,
    nu_ref,
    slice_ref,
    notional_ref,
    strike_ref,
    set_ref,
    factor_ref,
    loss_ref,
    back,
    totals,
    x_ref,
    shocks_ref,
    lt_ref,
    blocks,
    corr_ref,
    par,
    xs_send,
    xs,
    last_send,
    last,
    trades,
    states,
    parts,
    squashes,
    exposure,
    weights,
    terms,
    back_send,
    load,
    lt_send_sem,
    lt_recv_sem,
    lt_share_send,
    lt_share_recv,
    trade_send,
    trade_recv,
    trade_share_send,
    trade_share_recv,
    par_send,
    par_recv,
    path_send,
    path_recv,
    back_send_sem,
    back_recv_sem,
    total_send,
    total_recv,
):
    steps, width, path_cols = shocks_ref.shape
    groups = xs.shape[0]
    factors = corr_ref.shape[0]
    paths = path_cols // groups
    devices = totals.shape[0]
    path_groups = devices // groups
    sets = loss_ref.shape[1]
    slices = alpha_ref.shape[1]
    tile = trades.shape[4]
    pairs = steps // 2
    half = paths // 2
    bits = (sets - 1).bit_length()
    chunks = factors // LANES
    per_chunk = LANES // width

    me_f = lax.axis_index("factors")
    me_p = lax.axis_index("paths")
    share = me_p % SHARES
    share_base = me_p - share
    me = me_p * groups + me_f

    loads = [
        pltpu.make_async_copy(lt_hbm, lt_ref, load.at[0]),
        pltpu.make_async_copy(x_hbm, x_ref, load.at[1]),
        pltpu.make_async_copy(shocks_hbm, shocks_ref, load.at[2]),
    ]
    for copy in loads:
        copy.start()

    def device_at(d):
        if isinstance(d, tuple):
            return {"paths": (me_p + d[0]) % path_groups, "factors": (me_f + d[1]) % groups}
        return {"factors": (me_f + d) % groups}

    others = [(e, d) for e in range(path_groups) for d in range(groups) if e + d]
    barrier = pltpu.get_barrier_semaphore()
    for at in others:
        pl.semaphore_signal(barrier, inc=1, device_id=device_at(at), device_id_type=MESH)

    def owned(g):
        level = g // per_chunk
        before = pieces_before(g, per_chunk, chunks)
        step = (share - before % SHARES + SHARES) % SHARES
        return level + step, (before + step) // SHARES

    my_chunk, my_slot = owned(me_f)
    my_cols = pl.ds(pl.multiple_of(my_chunk % chunks * LANES, LANES), LANES)
    loads[0].wait()

    @pl.when(my_chunk < chunks)
    def _():
        blocks[share, my_slot] = lt_ref[:, my_cols].astype(BF16)

    slice_rows = lax.broadcasted_iota(jnp.int32, (slices, width), 0)
    picked = jnp.where(slice_rows == slice_ref[...], 1.0, 0.0)
    zero = jnp.zeros((5, slices), F32)
    smile = lax.dot_general(
        jnp.concatenate([alpha_ref[...], rho_ref[...], nu_ref[...], zero], axis=0),
        picked,
        NN,
        precision=PRECISE,
        preferred_element_type=F32,
    )
    par[me_f] = jnp.concatenate(
        [smile[:3], reversion_ref[...], slice_ref[...].astype(F32), smile[:3]], axis=0
    )
    loads[1].wait()
    loads[2].wait()
    xs_send[0] = jnp.concatenate([x_ref[...], shocks_ref[0]], axis=0).T.astype(BF16)
    for k in range(1, pairs):
        pair = jnp.concatenate([shocks_ref[2 * k - 1], shocks_ref[2 * k]], axis=0)
        xs_send[k] = pair.T.astype(BF16)
    final = shocks_ref[steps - 1].T
    for g in range(groups):
        top = g * paths
        last_send[g] = jnp.concatenate(
            [final[top : top + half], final[top + half : top + paths]], axis=1
        ).astype(BF16)
    mine = pl.ds(pl.multiple_of(me_f * paths, paths), paths)
    for k in range(pairs):
        xs[me_f, k] = xs_send[k, mine, :]
    last[me_f] = last_send[me_f]
    cols = pl.ds(pl.multiple_of(share * tile, tile), tile)
    code = set_ref[:, cols] + ((factor_ref[:, cols] - me_f * width) << bits)
    trades[share, me_f, 0] = notional_ref[:, cols]
    trades[share, me_f, 1] = strike_ref[:, cols]
    trades[share, me_f, 2] = code.astype(F32)

    pl.semaphore_wait(barrier, len(others))

    def remote(src, dst, send, recv, peer):
        return pltpu.make_async_remote_copy(
            src_ref=src, dst_ref=dst, send_sem=send, recv_sem=recv, device_id=peer, device_id_type=MESH
        )

    def before(d):
        return (me_f - d + groups) % groups

    def lt_copy(d, slot):
        ref = blocks.at[share, slot]
        return remote(ref, ref, lt_send_sem.at[d], lt_recv_sem.at[d], device_at(d))

    def shared_copy(ref, d, send, recv, at):
        peer = {"paths": share_base + (share + d) % SHARES}
        return remote(ref.at[at], ref.at[at], send.at[d], recv.at[d], peer)

    def lt_share(d, at):
        return shared_copy(blocks, d, lt_share_send, lt_share_recv, at)

    def trade_share(d, at):
        return shared_copy(trades, d, trade_share_send, trade_share_recv, at)

    def trade_copy(d, at):
        ref = trades.at[share, at]
        return remote(ref, ref, trade_send.at[d], trade_recv.at[d], device_at(d))

    def par_copy(d, at):
        return remote(par.at[at], par.at[at], par_send.at[d], par_recv.at[d], device_at(d))

    def path_copy(k, d, at):
        peer = (me_f + d) % groups
        if k < pairs:
            theirs = pl.ds(pl.multiple_of(peer * paths, paths), paths)
            src, dst = xs_send.at[k, theirs], xs.at[at, k]
        else:
            src, dst = last_send.at[peer], last.at[at]
        return remote(src, dst, path_send.at[k, d], path_recv.at[k, d], device_at(d))

    sent = []

    def start(copy):
        copy.start()
        sent.append(copy)

    away = range(1, groups)

    @pl.when(my_chunk < chunks)
    def _():
        for d in away:
            lt_copy(d, my_slot).start()

    for d in away:
        start(par_copy(d, me_f))
    for k in range(pairs):
        for d in away:
            start(path_copy(k, d, me_f))
    for d in away:
        start(trade_copy(d, me_f))
    for d in away:
        start(path_copy(pairs, d, me_f))

    for d in away:
        their_chunk, their_slot = owned(before(d))

        @pl.when(their_chunk < chunks)
        def _():
            lt_copy(d, their_slot).wait_recv()

    for d in range(1, SHARES):
        start(lt_share(d, share))

    for d in away:
        par_copy(d, before(d)).wait_recv()
    all_par = jnp.concatenate([par[g] for g in range(groups)], axis=1)
    alpha, rho, nu = all_par[0:1, :], all_par[1:2, :], all_par[2:3, :]
    damping = 1.0 - all_par[3:4, :] * TIME_STEP
    curve2 = 2.0 - 3.0 * rho * rho
    curve = curve2 * nu * nu / 24.0
    tilt = 0.5 * rho * nu

    def arrived(k):
        for d in away:
            path_copy(k, d, before(d)).wait_recv()
        if k < pairs:
            both = [xs[g, k].astype(F32) for g in range(groups)]
            return [
                jnp.concatenate([b[:, :width] for b in both], axis=1),
                jnp.concatenate([b[:, width:] for b in both], axis=1),
            ]
        both = [last[g].astype(F32) for g in range(groups)]
        return [
            jnp.concatenate(
                [
                    jnp.concatenate([b[:, :width] for b in both], axis=1),
                    jnp.concatenate([b[:, width:] for b in both], axis=1),
                ],
                axis=0,
            )
        ]

    state, shock = arrived(0)
    shocks = [shock]
    for d in range(1, SHARES):
        lt_share(d, (share - d + SHARES) % SHARES).wait_recv()
    empty = jnp.zeros((width, LANES), BF16)
    for g in range(groups):
        first = pieces_before(g, per_chunk, chunks)
        level = g // per_chunk
        for c in range(chunks):
            n = first + c - level
            corr_ref[g * width : (g + 1) * width, c * LANES : (c + 1) * LANES] = (
                empty if c < level else blocks[n % SHARES, n // SHARES]
            )

    ones = jnp.ones((paths, PAD), BF16)
    for k in range(steps):
        if k >= len(shocks):
            shocks.extend(arrived((k + 1) // 2))
        states[k] = state
        u = jnp.tanh(state)
        source = alpha * (1.0 + tilt * u + curve * u * u) * shocks[k]
        state = damping * state + ROOT_STEP * split_mm(source, corr_ref[...], NN)
        high, low = split(state)
        for b in range(groups):
            cols = slice(b * width, (b + 1) * width)
            parts[b, k * paths : (k + 1) * paths, :] = jnp.concatenate(
                [high[:, cols], low[:, cols], ones], axis=1
            )

    exposure[...] = jnp.zeros_like(exposure)

    def trade_rows(s, b):
        code = trades[s, b, 2].astype(jnp.int32)
        return trades[s, b, 0], trades[s, b, 1], code & ((1 << bits) - 1), code >> bits

    def forward(s, b, carry):
        notional, strike, in_set, factor = trade_rows(s, b)
        table = one_hot(factor, width)
        high, low = split(-strike)
        tail = jnp.concatenate([high, low, jnp.zeros((PAD - 2, tile), BF16)], axis=0)
        money = mm(parts[b], jnp.concatenate([table, table, tail], axis=0), NN)
        squash = jnp.tanh(money).astype(BF16)
        squashes[s, b] = squash
        exposure[...] += mm(squash, one_hot(in_set, sets, notional), NT)
        return carry

    for d in away:
        trade_copy(d, before(d)).wait_recv()
    for d in range(1, SHARES):
        start(trade_share(d, share))
    for d in range(SHARES):
        s = (share - d + SHARES) % SHARES
        if d:
            trade_share(d, s).wait_recv()
        lax.fori_loop(0, groups, functools.partial(forward, s), 0, unroll=UNROLL)

    for k in range(steps):
        at = slice(k * paths, (k + 1) * paths)
        scale = math.exp(-DISCOUNT_RATE * TIME_STEP * (k + 1)) * loss_ref[...]
        weights[at, :] = (scale * jax.nn.sigmoid(exposure[at, :])).astype(BF16)
    terms[...] = jnp.zeros_like(terms)

    def backward(i, carry):
        s, b = i % SHARES, i // SHARES
        notional, strike, in_set, factor = trade_rows(s, b)
        pulled = mm(weights[...], one_hot(in_set, sets), NN)
        squash = squashes[s, b].astype(F32)
        pulled = (pulled * (notional * (1.0 - squash * squash))).astype(BF16)
        terms[b] += mm(pulled, one_hot(factor, width), NT)
        return carry

    lax.fori_loop(0, SHARES * groups, backward, 0, unroll=UNROLL)

    adjoint = jnp.zeros((paths, factors), F32)
    sums = [jnp.zeros((1, factors), F32) for _ in range(3)]
    for k in reversed(range(steps)):
        adjoint = adjoint + jnp.concatenate(
            [terms[b, k * paths : (k + 1) * paths, :] for b in range(groups)], axis=1
        )
        u = jnp.tanh(states[k])
        vbar = split_mm(ROOT_STEP * adjoint, corr_ref[...], NT) * shocks[k]
        for at, slope in enumerate(
            (
                1.0 + tilt * u + curve * u * u,
                alpha * (0.5 * nu * u - 0.25 * rho * nu * nu * u * u),
                alpha * (0.5 * rho * u + curve2 * nu * u * u / 12.0),
            )
        ):
            sums[at] = sums[at] + jnp.sum(vbar * slope, axis=0, keepdims=True)
        adjoint = damping * adjoint + vbar * (alpha * (tilt + 2.0 * curve * u)) * (1.0 - u * u)

    folds = back.shape[2] // width
    depth = paths // folds
    for g in range(groups):
        cols = slice(g * width, (g + 1) * width)
        back_send[g] = jnp.concatenate(
            [adjoint[i * depth : (i + 1) * depth, cols] for i in range(folds)], axis=1
        )

    def back_copy(d, at):
        peer = (me_f + d) % groups
        return remote(back_send.at[peer], back.at[at], back_send_sem.at[d], back_recv_sem.at[d], device_at(d))

    def total_copy(n, at):
        return remote(totals.at[at], totals.at[at], total_send.at[n], total_recv.at[n], device_at(others[n]))

    for d in away:
        start(back_copy(d, me_f))
    back[me_f] = back_send[me_f]

    slice_rows = lax.broadcasted_iota(jnp.int32, (slices, factors), 0).astype(F32)
    slice_table = jnp.where(slice_rows == all_par[4:5, :], 1.0, 0.0)
    totals[me] = lax.dot_general(
        jnp.concatenate(sums + [jnp.zeros((5, factors), F32)], axis=0),
        slice_table,
        NT,
        precision=PRECISE,
        preferred_element_type=F32,
    )
    for n in range(len(others)):
        start(total_copy(n, me))

    @pl.when(my_chunk < chunks)
    def _():
        for d in away:
            lt_copy(d, my_slot).wait_send()

    for copy in sent:
        copy.wait_send()
    for d in away:
        back_copy(d, before(d)).wait_recv()
    for n, (e, d) in enumerate(others):
        at = (me_p - e + path_groups) % path_groups * groups + before(d)
        total_copy(n, at).wait_recv()


def finish_kernel(back_ref, totals_ref, a_ref, g_ref):
    groups, depth, lanes = back_ref.shape
    width = a_ref.shape[0]
    pieces = []
    for g in range(groups):
        piece = back_ref[g]
        pieces.extend(piece[:, i * width : (i + 1) * width] for i in range(lanes // width))
    a_ref[...] = jnp.concatenate(pieces, axis=0).T
    path_groups = totals_ref.shape[0] // groups
    g_ref[...] = jnp.sum(totals_ref[...], axis=0)[:3] / (a_ref.shape[1] * path_groups)


def per_device(
    x_start,
    shocks,
    cholesky,
    reversion,
    sabr_alpha,
    sabr_rho,
    sabr_nu,
    factor_slice,
    notional,
    strike,
    trade_set,
    trade_factor,
    loss_given,
):
    width, path_cols = x_start.shape
    steps, factors = shocks.shape[0], cholesky.shape[0]
    groups = lax.axis_size("factors")
    path_groups = lax.axis_size("paths")
    devices = groups * path_groups
    paths = path_cols // groups
    tile = notional.shape[0] // SHARES
    rows, sets, slices = steps * paths, loss_given.shape[0], sabr_alpha.shape[0]
    fold = LANES // width
    pairs = steps // 2
    slots = pieces_before(groups, fold, factors // LANES) // SHARES
    vmem, dma = pltpu.VMEM, pltpu.SemaphoreType.DMA
    whole = pl.BlockSpec(memory_space=pltpu.VMEM)
    back, totals = pl.pallas_call(
        fused_kernel,
        out_shape=(
            jax.ShapeDtypeStruct((groups, paths // fold, LANES), F32),
            jax.ShapeDtypeStruct((devices, 8, slices), F32),
        ),
        in_specs=[pl.BlockSpec(memory_space=pl.ANY)] * 3 + [whole] * 10,
        out_specs=(whole,) * 2,
        scratch_shapes=[
            vmem((width, path_cols), F32),
            vmem((steps, width, path_cols), F32),
            vmem((width, factors), F32),
            vmem((SHARES, slots, width, LANES), BF16),
            vmem((factors, factors), BF16),
            vmem((groups, 8, width), F32),
            vmem((pairs, path_cols, 2 * width), BF16),
            vmem((groups, pairs, paths, 2 * width), BF16),
            vmem((groups, paths // 2, 2 * width), BF16),
            vmem((groups, paths // 2, 2 * width), BF16),
            vmem((SHARES, groups, 3, 1, tile), F32),
            vmem((steps, paths, factors), F32),
            vmem((groups, rows, 2 * width + PAD), BF16),
            vmem((SHARES, groups, rows, tile), BF16),
            vmem((rows, sets), F32),
            vmem((rows, sets), BF16),
            vmem((groups, rows, width), F32),
            vmem((groups, paths // fold, LANES), F32),
            dma((3,)),
            dma((groups,)),
            dma((groups,)),
            dma((SHARES,)),
            dma((SHARES,)),
            dma((groups,)),
            dma((groups,)),
            dma((SHARES,)),
            dma((SHARES,)),
            dma((groups,)),
            dma((groups,)),
            dma((pairs + 1, groups)),
            dma((pairs + 1, groups)),
            dma((groups,)),
            dma((groups,)),
            dma((devices,)),
            dma((devices,)),
        ],
        compiler_params=pltpu.CompilerParams(
            collective_id=0, has_side_effects=True, vmem_limit_bytes=56 * 1024 * 1024
        ),
    )(
        x_start,
        shocks,
        cholesky.T,
        reversion[None, :],
        sabr_alpha[None, :],
        sabr_rho[None, :],
        sabr_nu[None, :],
        factor_slice[None, :],
        notional[None, :],
        strike[None, :],
        trade_set[None, :],
        trade_factor[None, :],
        loss_given[None, :],
    )
    return pl.pallas_call(
        finish_kernel,
        out_shape=(
            jax.ShapeDtypeStruct((width, path_cols), F32),
            jax.ShapeDtypeStruct((3, slices), F32),
        ),
        in_specs=[whole] * 2,
        out_specs=(whole,) * 2,
    )(back, totals)


def solution(mesh):
    return jax.shard_map(
        per_device,
        mesh=mesh,
        in_specs=(
            P("factors", "paths"),
            P(None, "factors", "paths"),
            P(None, "factors"),
            P("factors"),
            P(),
            P(),
            P(),
            P("factors"),
            P("factors"),
            P("factors"),
            P("factors"),
            P("factors"),
            P(),
        ),
        out_specs=(P("factors", "paths"), P()),
        check_vma=False,
    )
```

```python
import functools
import math

import jax
import jax.numpy as jnp
from jax import lax
from jax.experimental import pallas as pl
from jax.experimental.pallas import tpu as pltpu
from jax.sharding import PartitionSpec as P

TIME_STEP = 0.25
ROOT_STEP = 0.5
DISCOUNT_RATE = 0.03
PRECISE = lax.Precision.HIGHEST
MESH = pl.DeviceIdType.MESH
NN = (((1,), (0,)), ((), ()))
NT = (((1,), (1,)), ((), ()))
F32 = jnp.float32
BF16 = jnp.bfloat16
SHARES = 4
PAD = 16
LANES = 128
UNROLL = 8


def mm(a, b, dims):
    return lax.dot_general(a, b, dims, preferred_element_type=F32)


def split(a):
    high = a.astype(BF16)
    return high, (a - high.astype(F32)).astype(BF16)


def split3(a):
    high, rest = a.astype(BF16), a - a.astype(BF16).astype(F32)
    return (high,) + split(rest)


def split_mm(a, b, dims):
    rows = a.shape[0]
    both = mm(jnp.concatenate(split(a), axis=0), b, dims)
    return both[:rows] + both[rows:]


def one_hot(ids, count, value=None):
    shape = (count, ids.shape[1])
    rows = lax.broadcasted_iota(jnp.int16, shape, 0)
    value = jnp.ones((1, 1), BF16) if value is None else value.astype(BF16)
    hit = rows == jnp.broadcast_to(ids.astype(jnp.int16), shape)
    return jnp.where(hit, jnp.broadcast_to(value, shape), jnp.zeros(shape, BF16))


def pieces_before(g, per_chunk, chunks):
    level = g // per_chunk
    return per_chunk * (chunks * level - level * (level - 1) // 2) + g % per_chunk * (chunks - level)


def fused_kernel(
    x_hbm,
    shocks_hbm,
    lt_hbm,
    reversion_ref,
    alpha_ref,
    rho_ref,
    nu_ref,
    slice_ref,
    notional_ref,
    strike_ref,
    set_ref,
    factor_ref,
    loss_ref,
    back,
    totals,
    x_ref,
    shocks_ref,
    lt_ref,
    blocks,
    corr_ref,
    xs_send,
    xs,
    trades,
    states,
    parts,
    squashes,
    exposure,
    weights,
    terms,
    back_send,
    load,
    send_sems,
    recv_sems,
    share_sems,
):
    steps, width, path_cols = shocks_ref.shape
    groups = xs.shape[0]
    factors = corr_ref.shape[0]
    paths = path_cols // groups
    devices = totals.shape[0]
    path_groups = devices // groups
    sets = loss_ref.shape[1]
    slices = alpha_ref.shape[1]
    tile = trades.shape[4]
    pairs = steps // 2
    half = paths // 2
    slots = blocks.shape[1]
    bits = (sets - 1).bit_length()
    chunks = factors // LANES
    per_chunk = LANES // width

    me_f = lax.axis_index("factors")
    me_p = lax.axis_index("paths")
    share = me_p % SHARES
    share_base = me_p - share
    me = me_p * groups + me_f

    loads = [
        pltpu.make_async_copy(lt_hbm, lt_ref, load.at[0]),
        pltpu.make_async_copy(x_hbm, x_ref, load.at[1]),
        pltpu.make_async_copy(shocks_hbm, shocks_ref, load.at[2]),
    ]
    for copy in loads:
        copy.start()

    def device_at(d):
        if isinstance(d, tuple):
            return {"paths": (me_p + d[0]) % path_groups, "factors": (me_f + d[1]) % groups}
        return {"factors": (me_f + d) % groups}

    others = [(e, d) for e in range(path_groups) for d in range(groups) if e + d]
    barrier = pltpu.get_barrier_semaphore()
    for at in others:
        pl.semaphore_signal(barrier, inc=1, device_id=device_at(at), device_id_type=MESH)

    def owned(g):
        level = g // per_chunk
        before = pieces_before(g, per_chunk, chunks)
        step = (share - before % SHARES + SHARES) % SHARES
        return level + step, (before + step) // SHARES

    my_chunk, my_slot = owned(me_f)
    my_cols = pl.ds(pl.multiple_of(my_chunk % chunks * LANES, LANES), LANES)
    loads[0].wait()

    @pl.when(my_chunk < chunks)
    def _():
        blocks[share, my_slot] = lt_ref[:, my_cols].astype(BF16)

    slice_rows = lax.broadcasted_iota(jnp.int32, (slices, width), 0)
    picked = jnp.where(slice_rows == slice_ref[...], 1.0, 0.0)
    zero = jnp.zeros((5, slices), F32)
    smile = lax.dot_general(
        jnp.concatenate([alpha_ref[...], rho_ref[...], nu_ref[...], zero], axis=0),
        picked,
        NN,
        precision=PRECISE,
        preferred_element_type=F32,
    )
    smile = jnp.concatenate([smile[:3], reversion_ref[...]], axis=0)
    packed = jnp.concatenate(
        split3(smile) + (jnp.broadcast_to(slice_ref[...].astype(F32), smile.shape).astype(BF16),), axis=0
    )
    packed = jnp.concatenate([packed, packed], axis=1)
    loads[1].wait()
    loads[2].wait()
    columns = [jnp.concatenate([x_ref[...], shocks_ref[0]], axis=0).T.astype(BF16)]
    for k in range(1, pairs):
        columns.append(jnp.concatenate([shocks_ref[2 * k - 1], shocks_ref[2 * k]], axis=0).T.astype(BF16))
    final = shocks_ref[steps - 1].T
    for g in range(groups):
        top = g * paths
        for k in range(pairs):
            xs_send[g, k * paths : (k + 1) * paths] = columns[k][top : top + paths]
        xs_send[g, pairs * paths : pairs * paths + half] = jnp.concatenate(
            [final[top : top + half], final[top + half : top + paths]], axis=1
        ).astype(BF16)
        xs_send[g, pairs * paths + half :] = packed
    xs[me_f] = xs_send[me_f]
    cols = pl.ds(pl.multiple_of(share * tile, tile), tile)
    code = set_ref[:, cols] + ((factor_ref[:, cols] - me_f * width) << bits)
    trades[share, me_f, 0] = notional_ref[:, cols]
    trades[share, me_f, 1] = strike_ref[:, cols]
    trades[share, me_f, 2] = code.astype(F32)

    pl.semaphore_wait(barrier, len(others))

    def start(src, dst, kind, peer):
        pltpu.make_async_remote_copy(
            src_ref=src,
            dst_ref=dst,
            send_sem=send_sems.at[kind],
            recv_sem=recv_sems.at[kind],
            device_id=peer,
            device_id_type=MESH,
        ).start()

    def wait(ref, sem):
        pltpu.make_async_copy(ref, ref, sem).wait()

    away = range(1, groups)
    rest = pl.ds(0, groups - 1)

    @pl.when(my_chunk < chunks)
    def _():
        for d in away:
            start(blocks.at[share, my_slot], blocks.at[share, my_slot], 0, device_at(d))

    for d in away:
        start(trades.at[share, me_f], trades.at[share, me_f], 1, device_at(d))
    for d in away:
        start(xs_send.at[(me_f + d) % groups], xs.at[me_f], 2, device_at(d))

    @pl.when(my_chunk < chunks)
    def _():
        wait(blocks.at[share, pl.ds(0, slots - 1)], recv_sems.at[0])

    @pl.when(my_chunk >= chunks)
    def _():
        wait(blocks.at[share], recv_sems.at[0])

    def start_share(ref, kind):
        for d in range(1, SHARES):
            peer = {"paths": share_base + (share + d) % SHARES}
            pltpu.make_async_remote_copy(
                src_ref=ref.at[share],
                dst_ref=ref.at[share],
                send_sem=send_sems.at[kind],
                recv_sem=share_sems.at[kind - 3, d],
                device_id=peer,
                device_id_type=MESH,
            ).start()

    start_share(blocks, 3)
    wait(trades.at[share, rest], recv_sems.at[1])
    start_share(trades, 4)
    wait(xs.at[rest], recv_sems.at[2])

    low_rows = pairs * paths + half
    both = [xs[g].astype(F32) for g in range(groups)]
    lefts = jnp.concatenate([b[:, :width] for b in both], axis=1)
    rights = jnp.concatenate([b[:, width:] for b in both], axis=1)
    packed = lefts[low_rows:]
    all_par = packed[0:4] + (packed[4:8] + packed[8:12])
    slice_ids = packed[12:13]
    slice_rows = lax.broadcasted_iota(jnp.int32, (slices, factors), 0).astype(F32)
    slice_table = jnp.where(slice_rows == slice_ids, 1.0, 0.0).astype(BF16)
    state = lefts[:paths]
    shocks = [rights[:paths]]
    for k in range(1, pairs):
        shocks.extend([lefts[k * paths : (k + 1) * paths], rights[k * paths : (k + 1) * paths]])
    shocks.append(
        jnp.concatenate([lefts[pairs * paths : low_rows], rights[pairs * paths : low_rows]], axis=0)
    )
    alpha, rho, nu = all_par[0:1, :], all_par[1:2, :], all_par[2:3, :]
    damping = 1.0 - all_par[3:4, :] * TIME_STEP
    curve2 = 2.0 - 3.0 * rho * rho
    curve = curve2 * nu * nu / 24.0
    tilt = 0.5 * rho * nu

    for d in range(1, SHARES):
        wait(blocks.at[(share - d + SHARES) % SHARES], share_sems.at[0, d])
    empty = jnp.zeros((width, LANES), BF16)
    for g in range(groups):
        first = pieces_before(g, per_chunk, chunks)
        level = g // per_chunk
        for c in range(chunks):
            n = first + c - level
            corr_ref[g * width : (g + 1) * width, c * LANES : (c + 1) * LANES] = (
                empty if c < level else blocks[n % SHARES, n // SHARES]
            )

    ones = jnp.ones((paths, PAD), BF16)
    for k in range(steps):
        states[k] = state
        u = jnp.tanh(state)
        source = alpha * (1.0 + tilt * u + curve * u * u) * shocks[k]
        state = damping * state + ROOT_STEP * split_mm(source, corr_ref[...], NN)
        high, low = split(state)
        for b in range(groups):
            cols = slice(b * width, (b + 1) * width)
            parts[b, k * paths : (k + 1) * paths, :] = jnp.concatenate(
                [high[:, cols], low[:, cols], ones], axis=1
            )

    exposure[...] = jnp.zeros_like(exposure)

    def trade_rows(s, b):
        code = trades[s, b, 2].astype(jnp.int32)
        return trades[s, b, 0], trades[s, b, 1], code & ((1 << bits) - 1), code >> bits

    def forward(s, b, carry):
        notional, strike, in_set, factor = trade_rows(s, b)
        table = one_hot(factor, width)
        high, low = split(-strike)
        tail = jnp.concatenate([high, low, jnp.zeros((PAD - 2, tile), BF16)], axis=0)
        money = mm(parts[b], jnp.concatenate([table, table, tail], axis=0), NN)
        squash = jnp.tanh(money).astype(BF16)
        squashes[s, b] = squash
        exposure[...] += mm(squash, one_hot(in_set, sets, notional), NT)
        return carry

    def forward_share(d, carry):
        s = (share - d + SHARES) % SHARES

        @pl.when(d > 0)
        def _():
            wait(trades.at[s], share_sems.at[1, d])

        return lax.fori_loop(0, groups, functools.partial(forward, s), carry, unroll=UNROLL)

    lax.fori_loop(0, SHARES, forward_share, 0)

    for k in range(steps):
        at = slice(k * paths, (k + 1) * paths)
        scale = math.exp(-DISCOUNT_RATE * TIME_STEP * (k + 1)) * loss_ref[...]
        weights[at, :] = (scale * jax.nn.sigmoid(exposure[at, :])).astype(BF16)
    terms[...] = jnp.zeros_like(terms)

    def backward(i, carry):
        s, b = i % SHARES, i // SHARES
        notional, strike, in_set, factor = trade_rows(s, b)
        pulled = mm(weights[...], one_hot(in_set, sets), NN)
        squash = squashes[s, b].astype(F32)
        pulled = (pulled * (notional * (1.0 - squash * squash))).astype(BF16)
        terms[b] += mm(pulled, one_hot(factor, width), NT)
        return carry

    lax.fori_loop(0, SHARES * groups, backward, 0, unroll=UNROLL)

    adjoint = jnp.zeros((paths, factors), F32)
    sums = [jnp.zeros((1, factors), F32) for _ in range(3)]
    for k in reversed(range(steps)):
        adjoint = adjoint + jnp.concatenate(
            [terms[b, k * paths : (k + 1) * paths, :] for b in range(groups)], axis=1
        )
        u = jnp.tanh(states[k])
        vbar = split_mm(ROOT_STEP * adjoint, corr_ref[...], NT) * shocks[k]
        for at, slope in enumerate(
            (
                1.0 + tilt * u + curve * u * u,
                alpha * (0.5 * nu * u - 0.25 * rho * nu * nu * u * u),
                alpha * (0.5 * rho * u + curve2 * nu * u * u / 12.0),
            )
        ):
            sums[at] = sums[at] + jnp.sum(vbar * slope, axis=0, keepdims=True)
        adjoint = damping * adjoint + vbar * (alpha * (tilt + 2.0 * curve * u)) * (1.0 - u * u)

    folds = back.shape[2] // width
    depth = paths // folds
    for g in range(groups):
        cols = slice(g * width, (g + 1) * width)
        back_send[g] = jnp.concatenate(
            [adjoint[i * depth : (i + 1) * depth, cols] for i in range(folds)], axis=1
        )

    for d in away:
        start(back_send.at[(me_f + d) % groups], back.at[me_f], 5, device_at(d))
    back[me_f] = back_send[me_f]
    stacked = jnp.concatenate(sums + [jnp.zeros((5, factors), F32)], axis=0)
    thirds = mm(jnp.concatenate(split3(stacked), axis=0), slice_table, NT)
    totals[me] = thirds[0:8] + (thirds[8:16] + thirds[16:24])
    for at in others:
        start(totals.at[me], totals.at[me], 6, device_at(at))

    @pl.when(my_chunk < chunks)
    def _():
        for _ in away:
            wait(blocks.at[share, my_slot], send_sems.at[0])

    wait(trades.at[share, rest], send_sems.at[1])
    wait(xs.at[rest], send_sems.at[2])
    for d in range(1, SHARES):
        wait(blocks.at[share], send_sems.at[3])
        wait(trades.at[share], send_sems.at[4])
    wait(back.at[rest], send_sems.at[5])
    wait(totals.at[pl.ds(0, len(others))], send_sems.at[6])
    wait(back.at[rest], recv_sems.at[5])
    wait(totals.at[pl.ds(0, len(others))], recv_sems.at[6])


def finish_kernel(back_ref, totals_ref, a_ref, g_ref):
    groups, depth, lanes = back_ref.shape
    width = a_ref.shape[0]
    pieces = []
    for g in range(groups):
        piece = back_ref[g]
        pieces.extend(piece[:, i * width : (i + 1) * width] for i in range(lanes // width))
    a_ref[...] = jnp.concatenate(pieces, axis=0).T
    path_groups = totals_ref.shape[0] // groups
    g_ref[...] = jnp.sum(totals_ref[...], axis=0)[:3] / (a_ref.shape[1] * path_groups)


def per_device(
    x_start,
    shocks,
    cholesky,
    reversion,
    sabr_alpha,
    sabr_rho,
    sabr_nu,
    factor_slice,
    notional,
    strike,
    trade_set,
    trade_factor,
    loss_given,
):
    width, path_cols = x_start.shape
    steps, factors = shocks.shape[0], cholesky.shape[0]
    groups = lax.axis_size("factors")
    path_groups = lax.axis_size("paths")
    devices = groups * path_groups
    paths = path_cols // groups
    tile = notional.shape[0] // SHARES
    rows, sets, slices = steps * paths, loss_given.shape[0], sabr_alpha.shape[0]
    fold = LANES // width
    pairs = steps // 2
    path_rows = pairs * paths + paths // 2 + 16
    slots = pieces_before(groups, fold, factors // LANES) // SHARES
    vmem, dma = pltpu.VMEM, pltpu.SemaphoreType.DMA
    whole = pl.BlockSpec(memory_space=pltpu.VMEM)
    back, totals = pl.pallas_call(
        fused_kernel,
        out_shape=(
            jax.ShapeDtypeStruct((groups, paths // fold, LANES), F32),
            jax.ShapeDtypeStruct((devices, 8, slices), F32),
        ),
        in_specs=[pl.BlockSpec(memory_space=pl.ANY)] * 3 + [whole] * 10,
        out_specs=(whole,) * 2,
        scratch_shapes=[
            vmem((width, path_cols), F32),
            vmem((steps, width, path_cols), F32),
            vmem((width, factors), F32),
            vmem((SHARES, slots, width, LANES), BF16),
            vmem((factors, factors), BF16),
            vmem((groups, path_rows, 2 * width), BF16),
            vmem((groups, path_rows, 2 * width), BF16),
            vmem((SHARES, groups, 3, 1, tile), F32),
            vmem((steps, paths, factors), F32),
            vmem((groups, rows, 2 * width + PAD), BF16),
            vmem((SHARES, groups, rows, tile), BF16),
            vmem((rows, sets), F32),
            vmem((rows, sets), BF16),
            vmem((groups, rows, width), F32),
            vmem((groups, paths // fold, LANES), F32),
            dma((3,)),
            dma((7,)),
            dma((7,)),
            dma((2, SHARES)),
        ],
        compiler_params=pltpu.CompilerParams(
            collective_id=0, has_side_effects=True, vmem_limit_bytes=56 * 1024 * 1024
        ),
    )(
        x_start,
        shocks,
        cholesky.T,
        reversion[None, :],
        sabr_alpha[None, :],
        sabr_rho[None, :],
        sabr_nu[None, :],
        factor_slice[None, :],
        notional[None, :],
        strike[None, :],
        trade_set[None, :],
        trade_factor[None, :],
        loss_given[None, :],
    )
    return pl.pallas_call(
        finish_kernel,
        out_shape=(
            jax.ShapeDtypeStruct((width, path_cols), F32),
            jax.ShapeDtypeStruct((3, slices), F32),
        ),
        in_specs=[whole] * 2,
        out_specs=(whole,) * 2,
    )(back, totals)


def solution(mesh):
    return jax.shard_map(
        per_device,
        mesh=mesh,
        in_specs=(
            P("factors", "paths"),
            P(None, "factors", "paths"),
            P(None, "factors"),
            P("factors"),
            P(),
            P(),
            P(),
            P("factors"),
            P("factors"),
            P("factors"),
            P("factors"),
            P("factors"),
            P(),
        ),
        out_specs=(P("factors", "paths"), P()),
        check_vma=False,
    )
```

```python
import functools
import math

import jax
import jax.numpy as jnp
from jax import lax
from jax.experimental import pallas as pl
from jax.experimental.pallas import tpu as pltpu
from jax.sharding import PartitionSpec as P

TIME_STEP = 0.25
ROOT_STEP = 0.5
DISCOUNT_RATE = 0.03
PRECISE = lax.Precision.HIGHEST
MESH = pl.DeviceIdType.MESH
NN = (((1,), (0,)), ((), ()))
NT = (((1,), (1,)), ((), ()))
F32 = jnp.float32
BF16 = jnp.bfloat16
SHARES = 4
PAD = 16
LANES = 128
UNROLL = 8


def mm(a, b, dims):
    return lax.dot_general(a, b, dims, preferred_element_type=F32)


def split(a):
    high = a.astype(BF16)
    return high, (a - high.astype(F32)).astype(BF16)


def split3(a):
    high, rest = a.astype(BF16), a - a.astype(BF16).astype(F32)
    return (high,) + split(rest)


def split_mm(a, b, dims):
    rows = a.shape[0]
    both = mm(jnp.concatenate(split(a), axis=0), b, dims)
    return both[:rows] + both[rows:]


def one_hot(ids, count, value=None):
    shape = (count, ids.shape[1])
    rows = lax.broadcasted_iota(jnp.int16, shape, 0)
    value = jnp.ones((1, 1), BF16) if value is None else value.astype(BF16)
    hit = rows == jnp.broadcast_to(ids.astype(jnp.int16), shape)
    return jnp.where(hit, jnp.broadcast_to(value, shape), jnp.zeros(shape, BF16))


def pieces_before(g, per_chunk, chunks):
    level = g // per_chunk
    return per_chunk * (chunks * level - level * (level - 1) // 2) + g % per_chunk * (chunks - level)


def fused_kernel(
    x_hbm,
    shocks_hbm,
    lt_hbm,
    reversion_ref,
    alpha_ref,
    rho_ref,
    nu_ref,
    slice_ref,
    notional_ref,
    strike_ref,
    set_ref,
    factor_ref,
    loss_ref,
    back,
    totals,
    x_ref,
    shocks_ref,
    lt_ref,
    blocks,
    corr_ref,
    xs_send,
    xs,
    trades,
    states,
    parts,
    squashes,
    exposure,
    weights,
    terms,
    back_send,
    load,
    send_sems,
    recv_sems,
    share_sems,
):
    steps, width, path_cols = shocks_ref.shape
    groups = xs.shape[0]
    factors = corr_ref.shape[0]
    paths = path_cols // groups
    devices = totals.shape[0]
    path_groups = devices // groups
    sets = loss_ref.shape[1]
    slices = alpha_ref.shape[1]
    tile = trades.shape[4]
    pairs = steps // 2
    half = paths // 2
    slots = blocks.shape[1]
    bits = (sets - 1).bit_length()
    chunks = factors // LANES
    per_chunk = LANES // width

    me_f = lax.axis_index("factors")
    me_p = lax.axis_index("paths")
    share = me_p % SHARES
    share_base = me_p - share
    me = me_p * groups + me_f

    loads = [
        pltpu.make_async_copy(lt_hbm, lt_ref, load.at[0]),
        pltpu.make_async_copy(x_hbm, x_ref, load.at[1]),
        pltpu.make_async_copy(shocks_hbm, shocks_ref, load.at[2]),
    ]
    for copy in loads:
        copy.start()

    def device_at(d):
        if isinstance(d, tuple):
            return {"paths": (me_p + d[0]) % path_groups, "factors": (me_f + d[1]) % groups}
        return {"factors": (me_f + d) % groups}

    others = [(e, d) for e in range(path_groups) for d in range(groups) if e + d]
    barrier = pltpu.get_barrier_semaphore()
    for at in others:
        pl.semaphore_signal(barrier, inc=1, device_id=device_at(at), device_id_type=MESH)

    def owned(g):
        level = g // per_chunk
        before = pieces_before(g, per_chunk, chunks)
        step = (share - before % SHARES + SHARES) % SHARES
        return level + step, (before + step) // SHARES

    my_chunk, my_slot = owned(me_f)
    my_cols = pl.ds(pl.multiple_of(my_chunk % chunks * LANES, LANES), LANES)
    loads[0].wait()

    @pl.when(my_chunk < chunks)
    def _():
        blocks[share, my_slot] = lt_ref[:, my_cols].astype(BF16)

    pl.semaphore_wait(barrier, len(others))

    def start(src, dst, kind, peer):
        pltpu.make_async_remote_copy(
            src_ref=src,
            dst_ref=dst,
            send_sem=send_sems.at[kind],
            recv_sem=recv_sems.at[kind],
            device_id=peer,
            device_id_type=MESH,
        ).start()

    def wait(ref, sem):
        pltpu.make_async_copy(ref, ref, sem).wait()

    away = range(1, groups)
    rest = pl.ds(0, groups - 1)

    @pl.when(my_chunk < chunks)
    def _():
        for d in away:
            start(blocks.at[share, my_slot], blocks.at[share, my_slot], 0, device_at(d))

    slice_rows = lax.broadcasted_iota(jnp.int32, (slices, width), 0)
    picked = jnp.where(slice_rows == slice_ref[...], 1.0, 0.0)
    zero = jnp.zeros((5, slices), F32)
    smile = lax.dot_general(
        jnp.concatenate([alpha_ref[...], rho_ref[...], nu_ref[...], zero], axis=0),
        picked,
        NN,
        precision=PRECISE,
        preferred_element_type=F32,
    )
    smile = jnp.concatenate([smile[:3], reversion_ref[...]], axis=0)
    packed = jnp.concatenate(
        split3(smile) + (jnp.broadcast_to(slice_ref[...].astype(F32), smile.shape).astype(BF16),), axis=0
    )
    packed = jnp.concatenate([packed, packed], axis=1)
    loads[1].wait()
    loads[2].wait()
    columns = [jnp.concatenate([x_ref[...], shocks_ref[0]], axis=0).T.astype(BF16)]
    for k in range(1, pairs):
        columns.append(jnp.concatenate([shocks_ref[2 * k - 1], shocks_ref[2 * k]], axis=0).T.astype(BF16))
    final = shocks_ref[steps - 1].T
    for g in range(groups):
        top = g * paths
        for k in range(pairs):
            xs_send[g, k * paths : (k + 1) * paths] = columns[k][top : top + paths]
        xs_send[g, pairs * paths : pairs * paths + half] = jnp.concatenate(
            [final[top : top + half], final[top + half : top + paths]], axis=1
        ).astype(BF16)
        xs_send[g, pairs * paths + half :] = packed
    xs[me_f] = xs_send[me_f]
    for d in away:
        start(xs_send.at[(me_f + d) % groups], xs.at[me_f], 2, device_at(d))

    for n in range(SHARES):
        cols = slice(n * tile, (n + 1) * tile)
        code = set_ref[:, cols] + ((factor_ref[:, cols] - me_f * width) << bits)
        trades[n, groups, 0] = notional_ref[:, cols]
        trades[n, groups, 1] = strike_ref[:, cols]
        trades[n, groups, 2] = code.astype(F32)
    trades[share, me_f] = trades[share, groups]
    for d in away:
        start(trades.at[share, me_f], trades.at[share, me_f], 1, device_at(d))

    @pl.when(my_chunk < chunks)
    def _():
        wait(blocks.at[share, pl.ds(0, slots - 1)], recv_sems.at[0])

    @pl.when(my_chunk >= chunks)
    def _():
        wait(blocks.at[share], recv_sems.at[0])

    def start_share(ref, kind):
        for d in range(1, SHARES):
            peer = {"paths": share_base + (share + d) % SHARES}
            pltpu.make_async_remote_copy(
                src_ref=ref,
                dst_ref=ref,
                send_sem=send_sems.at[kind],
                recv_sem=share_sems.at[kind - 3, d],
                device_id=peer,
                device_id_type=MESH,
            ).start()

    start_share(blocks.at[share], 3)
    wait(xs.at[rest], recv_sems.at[2])

    low_rows = pairs * paths + half
    both = [xs[g].astype(F32) for g in range(groups)]
    lefts = jnp.concatenate([b[:, :width] for b in both], axis=1)
    rights = jnp.concatenate([b[:, width:] for b in both], axis=1)
    packed = lefts[low_rows:]
    all_par = packed[0:4] + (packed[4:8] + packed[8:12])
    slice_ids = packed[12:13]
    slice_rows = lax.broadcasted_iota(jnp.int32, (slices, factors), 0).astype(F32)
    slice_table = jnp.where(slice_rows == slice_ids, 1.0, 0.0).astype(BF16)
    state = lefts[:paths]
    shocks = [rights[:paths]]
    for k in range(1, pairs):
        shocks.extend([lefts[k * paths : (k + 1) * paths], rights[k * paths : (k + 1) * paths]])
    shocks.append(
        jnp.concatenate([lefts[pairs * paths : low_rows], rights[pairs * paths : low_rows]], axis=0)
    )
    alpha, rho, nu = all_par[0:1, :], all_par[1:2, :], all_par[2:3, :]
    damping = 1.0 - all_par[3:4, :] * TIME_STEP
    curve2 = 2.0 - 3.0 * rho * rho
    curve = curve2 * nu * nu / 24.0
    tilt = 0.5 * rho * nu

    for d in range(1, SHARES):
        wait(blocks.at[(share - d + SHARES) % SHARES], share_sems.at[0, d])
    empty = jnp.zeros((width, LANES), BF16)
    for g in range(groups):
        first = pieces_before(g, per_chunk, chunks)
        level = g // per_chunk
        for c in range(chunks):
            n = first + c - level
            corr_ref[g * width : (g + 1) * width, c * LANES : (c + 1) * LANES] = (
                empty if c < level else blocks[n % SHARES, n // SHARES]
            )

    ones = jnp.ones((paths, PAD), BF16)
    for k in range(steps):
        states[k] = state
        u = jnp.tanh(state)
        source = alpha * (1.0 + tilt * u + curve * u * u) * shocks[k]
        state = damping * state + ROOT_STEP * split_mm(source, corr_ref[...], NN)
        high, low = split(state)
        for b in range(groups):
            cols = slice(b * width, (b + 1) * width)
            parts[b, k * paths : (k + 1) * paths, :] = jnp.concatenate(
                [high[:, cols], low[:, cols], ones], axis=1
            )

    exposure[...] = jnp.zeros_like(exposure)

    def trade_rows(s, b):
        code = trades[s, b, 2].astype(jnp.int32)
        return trades[s, b, 0], trades[s, b, 1], code & ((1 << bits) - 1), code >> bits

    def forward(s, slot, b, carry):
        notional, strike, in_set, factor = trade_rows(s, slot)
        table = one_hot(factor, width)
        high, low = split(-strike)
        tail = jnp.concatenate([high, low, jnp.zeros((PAD - 2, tile), BF16)], axis=0)
        money = mm(parts[b], jnp.concatenate([table, table, tail], axis=0), NN)
        squash = jnp.tanh(money).astype(BF16)
        squashes[s, b] = squash
        exposure[...] += mm(squash, one_hot(in_set, sets, notional), NT)
        return carry

    every = pl.ds(0, groups)
    wait(trades.at[share, rest], recv_sems.at[1])
    start_share(trades.at[share, every], 4)
    lax.fori_loop(0, SHARES, lambda s, c: forward(s, groups, me_f, c), 0, unroll=SHARES)

    def forward_share(d, carry):
        s = (share - d + SHARES) % SHARES

        @pl.when(d > 0)
        def _():
            wait(trades.at[s, every], share_sems.at[1, d])

        def forward_other(n, carry):
            b = (me_f + n) % groups
            return forward(s, b, b, carry)

        return lax.fori_loop(1, groups, forward_other, carry, unroll=groups - 1)

    lax.fori_loop(0, SHARES, forward_share, 0)

    for k in range(steps):
        at = slice(k * paths, (k + 1) * paths)
        scale = math.exp(-DISCOUNT_RATE * TIME_STEP * (k + 1)) * loss_ref[...]
        weights[at, :] = (scale * jax.nn.sigmoid(exposure[at, :])).astype(BF16)
    terms[...] = jnp.zeros_like(terms)

    def backward(i, carry):
        s, b = i % SHARES, i // SHARES
        notional, strike, in_set, factor = trade_rows(s, b)
        pulled = mm(weights[...], one_hot(in_set, sets), NN)
        squash = squashes[s, b].astype(F32)
        pulled = (pulled * (notional * (1.0 - squash * squash))).astype(BF16)
        terms[b] += mm(pulled, one_hot(factor, width), NT)
        return carry

    lax.fori_loop(0, SHARES * groups, backward, 0, unroll=UNROLL)

    adjoint = jnp.zeros((paths, factors), F32)
    sums = [jnp.zeros((1, factors), F32) for _ in range(3)]
    for k in reversed(range(steps)):
        adjoint = adjoint + jnp.concatenate(
            [terms[b, k * paths : (k + 1) * paths, :] for b in range(groups)], axis=1
        )
        u = jnp.tanh(states[k])
        vbar = split_mm(ROOT_STEP * adjoint, corr_ref[...], NT) * shocks[k]
        for at, slope in enumerate(
            (
                1.0 + tilt * u + curve * u * u,
                alpha * (0.5 * nu * u - 0.25 * rho * nu * nu * u * u),
                alpha * (0.5 * rho * u + curve2 * nu * u * u / 12.0),
            )
        ):
            sums[at] = sums[at] + jnp.sum(vbar * slope, axis=0, keepdims=True)
        adjoint = damping * adjoint + vbar * (alpha * (tilt + 2.0 * curve * u)) * (1.0 - u * u)

    for g in range(groups):
        cols = slice(g * width, (g + 1) * width)
        back_send[g] = jnp.concatenate([adjoint[:half, cols], adjoint[half:, cols]], axis=1).astype(BF16)

    for d in away:
        start(back_send.at[(me_f + d) % groups], back.at[me_f], 5, device_at(d))
    back[me_f] = back_send[me_f]
    stacked = jnp.concatenate(sums + [jnp.zeros((5, factors), F32)], axis=0)
    thirds = mm(jnp.concatenate(split3(stacked), axis=0), slice_table, NT)
    rows = thirds[0:8] + (thirds[8:16] + thirds[16:24])
    totals[me] = jnp.concatenate([rows[n : n + 1] for n in range(4)], axis=1)
    for at in others:
        start(totals.at[me], totals.at[me], 6, device_at(at))

    @pl.when(my_chunk < chunks)
    def _():
        for _ in away:
            wait(blocks.at[share, my_slot], send_sems.at[0])

    wait(trades.at[share, rest], send_sems.at[1])
    wait(xs.at[rest], send_sems.at[2])
    for d in range(1, SHARES):
        wait(blocks.at[share], send_sems.at[3])
        wait(trades.at[share, every], send_sems.at[4])
    wait(back.at[rest], send_sems.at[5])
    wait(totals.at[pl.ds(0, len(others))], send_sems.at[6])
    wait(back.at[rest], recv_sems.at[5])
    wait(totals.at[pl.ds(0, len(others))], recv_sems.at[6])


def finish_kernel(back_ref, totals_ref, a_ref, g_ref):
    groups = back_ref.shape[0]
    width, path_cols = a_ref.shape
    slices = g_ref.shape[1]
    pieces = []
    for g in range(groups):
        piece = back_ref[g].astype(F32)
        pieces.extend([piece[:, :width], piece[:, width:]])
    a_ref[...] = jnp.concatenate(pieces, axis=0).T
    path_groups = totals_ref.shape[0] // groups
    total = jnp.sum(totals_ref[...], axis=0) / (path_cols * path_groups)
    g_ref[...] = jnp.concatenate([total[:, n * slices : (n + 1) * slices] for n in range(3)], axis=0)


def per_device(
    x_start,
    shocks,
    cholesky,
    reversion,
    sabr_alpha,
    sabr_rho,
    sabr_nu,
    factor_slice,
    notional,
    strike,
    trade_set,
    trade_factor,
    loss_given,
):
    width, path_cols = x_start.shape
    steps, factors = shocks.shape[0], cholesky.shape[0]
    groups = lax.axis_size("factors")
    path_groups = lax.axis_size("paths")
    devices = groups * path_groups
    paths = path_cols // groups
    tile = notional.shape[0] // SHARES
    rows, sets, slices = steps * paths, loss_given.shape[0], sabr_alpha.shape[0]
    fold = LANES // width
    pairs = steps // 2
    path_rows = pairs * paths + paths // 2 + 16
    slots = pieces_before(groups, fold, factors // LANES) // SHARES
    vmem, dma = pltpu.VMEM, pltpu.SemaphoreType.DMA
    whole = pl.BlockSpec(memory_space=pltpu.VMEM)
    back, totals = pl.pallas_call(
        fused_kernel,
        out_shape=(
            jax.ShapeDtypeStruct((groups, paths // 2, 2 * width), BF16),
            jax.ShapeDtypeStruct((devices, 1, 4 * slices), F32),
        ),
        in_specs=[pl.BlockSpec(memory_space=pl.ANY)] * 3 + [whole] * 10,
        out_specs=(whole,) * 2,
        scratch_shapes=[
            vmem((width, path_cols), F32),
            vmem((steps, width, path_cols), F32),
            vmem((width, factors), F32),
            vmem((SHARES, slots, width, LANES), BF16),
            vmem((factors, factors), BF16),
            vmem((groups, path_rows, 2 * width), BF16),
            vmem((groups, path_rows, 2 * width), BF16),
            vmem((SHARES, groups + 1, 3, 1, tile), F32),
            vmem((steps, paths, factors), F32),
            vmem((groups, rows, 2 * width + PAD), BF16),
            vmem((SHARES, groups, rows, tile), BF16),
            vmem((rows, sets), F32),
            vmem((rows, sets), BF16),
            vmem((groups, rows, width), F32),
            vmem((groups, paths // 2, 2 * width), BF16),
            dma((3,)),
            dma((7,)),
            dma((7,)),
            dma((2, SHARES)),
        ],
        compiler_params=pltpu.CompilerParams(
            collective_id=0, has_side_effects=True, vmem_limit_bytes=56 * 1024 * 1024
        ),
    )(
        x_start,
        shocks,
        cholesky.T,
        reversion[None, :],
        sabr_alpha[None, :],
        sabr_rho[None, :],
        sabr_nu[None, :],
        factor_slice[None, :],
        notional[None, :],
        strike[None, :],
        trade_set[None, :],
        trade_factor[None, :],
        loss_given[None, :],
    )
    return pl.pallas_call(
        finish_kernel,
        out_shape=(
            jax.ShapeDtypeStruct((width, path_cols), F32),
            jax.ShapeDtypeStruct((3, slices), F32),
        ),
        in_specs=[whole] * 2,
        out_specs=(whole,) * 2,
    )(back, totals)


def solution(mesh):
    return jax.shard_map(
        per_device,
        mesh=mesh,
        in_specs=(
            P("factors", "paths"),
            P(None, "factors", "paths"),
            P(None, "factors"),
            P("factors"),
            P(),
            P(),
            P(),
            P("factors"),
            P("factors"),
            P("factors"),
            P("factors"),
            P("factors"),
            P(),
        ),
        out_specs=(P("factors", "paths"), P()),
        check_vma=False,
    )
```

```python
import functools
import math

import jax
import jax.numpy as jnp
from jax import lax
from jax.experimental import pallas as pl
from jax.experimental.pallas import tpu as pltpu
from jax.sharding import PartitionSpec as P

TIME_STEP = 0.25
ROOT_STEP = 0.5
DISCOUNT_RATE = 0.03
PRECISE = lax.Precision.HIGHEST
MESH = pl.DeviceIdType.MESH
NN = (((1,), (0,)), ((), ()))
NT = (((1,), (1,)), ((), ()))
F32 = jnp.float32
BF16 = jnp.bfloat16
SHARES = 4
PAD = 16
LANES = 128
UNROLL = 8


def mm(a, b, dims):
    return lax.dot_general(a, b, dims, preferred_element_type=F32)


def split(a):
    high = a.astype(BF16)
    return high, (a - high.astype(F32)).astype(BF16)


def split3(a):
    high, rest = a.astype(BF16), a - a.astype(BF16).astype(F32)
    return (high,) + split(rest)


def split_mm(a, b, dims):
    rows = a.shape[0]
    both = mm(jnp.concatenate(split(a), axis=0), b, dims)
    return both[:rows] + both[rows:]


def one_hot(ids, count, value=None):
    shape = (count, ids.shape[1])
    rows = lax.broadcasted_iota(jnp.int16, shape, 0)
    value = jnp.ones((1, 1), BF16) if value is None else value.astype(BF16)
    hit = rows == jnp.broadcast_to(ids.astype(jnp.int16), shape)
    return jnp.where(hit, jnp.broadcast_to(value, shape), jnp.zeros(shape, BF16))


def pieces_before(g, per_chunk, chunks):
    level = g // per_chunk
    return per_chunk * (chunks * level - level * (level - 1) // 2) + g % per_chunk * (chunks - level)


def fused_kernel(
    x_hbm,
    shocks_hbm,
    lt_hbm,
    reversion_hbm,
    alpha_hbm,
    rho_hbm,
    nu_hbm,
    slice_hbm,
    notional_hbm,
    strike_hbm,
    set_hbm,
    factor_hbm,
    loss_hbm,
    back,
    totals,
    x_ref,
    shocks_ref,
    lt_ref,
    reversion_ref,
    alpha_ref,
    rho_ref,
    nu_ref,
    slice_ref,
    notional_ref,
    strike_ref,
    set_ref,
    factor_ref,
    loss_ref,
    par,
    blocks,
    corr_ref,
    xs_send,
    xs,
    trades,
    states,
    parts,
    squashes,
    exposure,
    weights,
    terms,
    back_send,
    load,
    send_sems,
    recv_sems,
    share_sems,
):
    steps, width, path_cols = shocks_ref.shape
    groups = xs.shape[0]
    factors = corr_ref.shape[0]
    paths = path_cols // groups
    devices = totals.shape[0]
    path_groups = devices // groups
    sets = loss_ref.shape[1]
    slices = alpha_ref.shape[1]
    tile = trades.shape[4]
    pairs = steps // 2
    half = paths // 2
    slots = blocks.shape[1]
    bits = (sets - 1).bit_length()
    chunks = factors // LANES
    per_chunk = LANES // width

    me_f = lax.axis_index("factors")
    me_p = lax.axis_index("paths")
    share = me_p % SHARES
    share_base = me_p - share
    me = me_p * groups + me_f

    pairs_in = [
        (lt_hbm, lt_ref),
        (reversion_hbm, reversion_ref),
        (slice_hbm, slice_ref),
        (x_hbm, x_ref),
        (shocks_hbm, shocks_ref),
        (notional_hbm, notional_ref),
        (strike_hbm, strike_ref),
        (set_hbm, set_ref),
        (factor_hbm, factor_ref),
        (alpha_hbm, alpha_ref),
        (rho_hbm, rho_ref),
        (nu_hbm, nu_ref),
        (loss_hbm, loss_ref),
    ]
    loads = [
        pltpu.make_async_copy(src, dst, load.at[n]) for n, (src, dst) in enumerate(pairs_in)
    ]

    def loaded(*which):
        for n in which:
            loads[n].wait()

    loads[0].start()

    def device_at(d):
        if isinstance(d, tuple):
            return {"paths": (me_p + d[0]) % path_groups, "factors": (me_f + d[1]) % groups}
        return {"factors": (me_f + d) % groups}

    others = [(e, d) for e in range(path_groups) for d in range(groups) if e + d]
    barrier = pltpu.get_barrier_semaphore()
    near = [(e, d) for e, d in others if e == 0 or d == 0]
    for at in near:
        pl.semaphore_signal(barrier, inc=1, device_id=device_at(at), device_id_type=MESH)
    for copy in loads[1:]:
        copy.start()

    def owned(g):
        level = g // per_chunk
        before = pieces_before(g, per_chunk, chunks)
        step = (share - before % SHARES + SHARES) % SHARES
        return level + step, (before + step) // SHARES

    my_chunk, my_slot = owned(me_f)
    my_cols = pl.ds(pl.multiple_of(my_chunk % chunks * LANES, LANES), LANES)
    loaded(0)

    @pl.when(my_chunk < chunks)
    def _():
        blocks[share, my_slot] = lt_ref[:, my_cols].astype(BF16)

    loaded(1, 2)
    par[me_f] = jnp.concatenate([reversion_ref[...], slice_ref[...].astype(F32)], axis=1)
    pl.semaphore_wait(barrier, len(near))

    def start(src, dst, kind, peer):
        pltpu.make_async_remote_copy(
            src_ref=src,
            dst_ref=dst,
            send_sem=send_sems.at[kind],
            recv_sem=recv_sems.at[kind],
            device_id=peer,
            device_id_type=MESH,
        ).start()

    def wait(ref, sem):
        pltpu.make_async_copy(ref, ref, sem).wait()

    away = range(1, groups)
    rest = pl.ds(0, groups - 1)

    @pl.when(my_chunk < chunks)
    def _():
        for d in away:
            start(blocks.at[share, my_slot], blocks.at[share, my_slot], 0, device_at(d))

    for d in away:
        start(par.at[me_f], par.at[me_f], 7, device_at(d))
    loaded(3, 4)
    columns = [jnp.concatenate([x_ref[...], shocks_ref[0]], axis=0).astype(BF16).T]
    for k in range(1, pairs):
        pair = jnp.concatenate([shocks_ref[2 * k - 1], shocks_ref[2 * k]], axis=0)
        columns.append(pair.astype(BF16).T)
    final = shocks_ref[steps - 1].astype(BF16).T
    for g in range(groups):
        top = g * paths
        for k in range(pairs):
            xs_send[g, k * paths : (k + 1) * paths] = columns[k][top : top + paths]
        xs_send[g, pairs * paths :] = jnp.concatenate(
            [final[top : top + half], final[top + half : top + paths]], axis=1
        )
    xs[me_f] = xs_send[me_f]
    for d in away:
        start(xs_send.at[(me_f + d) % groups], xs.at[me_f], 2, device_at(d))

    loaded(5, 6, 7, 8)
    for n in range(SHARES):
        cols = slice(n * tile, (n + 1) * tile)
        code = set_ref[:, cols] + ((factor_ref[:, cols] - me_f * width) << bits)
        trades[n, groups, 0] = notional_ref[:, cols]
        trades[n, groups, 1] = strike_ref[:, cols]
        trades[n, groups, 2] = code.astype(F32)
    trades[share, me_f] = trades[share, groups]
    for d in away:
        start(trades.at[share, me_f], trades.at[share, me_f], 1, device_at(d))

    @pl.when(my_chunk < chunks)
    def _():
        wait(blocks.at[share, pl.ds(0, slots - 1)], recv_sems.at[0])

    @pl.when(my_chunk >= chunks)
    def _():
        wait(blocks.at[share], recv_sems.at[0])

    def start_share(ref, kind):
        for d in range(1, SHARES):
            peer = {"paths": share_base + (share + d) % SHARES}
            pltpu.make_async_remote_copy(
                src_ref=ref,
                dst_ref=ref,
                send_sem=send_sems.at[kind],
                recv_sem=share_sems.at[kind - 3, d],
                device_id=peer,
                device_id_type=MESH,
            ).start()

    start_share(blocks.at[share], 3)
    loaded(9, 10, 11, 12)
    wait(par.at[rest], recv_sems.at[7])
    all_par = [par[g] for g in range(groups)]
    damping = 1.0 - jnp.concatenate([p[:, :width] for p in all_par], axis=1) * TIME_STEP
    slice_ids = jnp.concatenate([p[:, width:] for p in all_par], axis=1)
    slice_rows = lax.broadcasted_iota(jnp.int32, (slices, factors), 0).astype(F32)
    slice_table = jnp.where(slice_rows == slice_ids, 1.0, 0.0).astype(BF16)
    smile = jnp.concatenate(
        [alpha_ref[...], rho_ref[...], nu_ref[...], jnp.zeros((5, slices), F32)], axis=0
    )
    smile = mm(jnp.concatenate(split3(smile), axis=0), slice_table, NN)
    smile = smile[0:8] + (smile[8:16] + smile[16:24])
    alpha, rho, nu = smile[0:1, :], smile[1:2, :], smile[2:3, :]
    curve2 = 2.0 - 3.0 * rho * rho
    curve = curve2 * nu * nu / 24.0
    tilt = 0.5 * rho * nu

    for d in range(1, SHARES):
        wait(blocks.at[(share - d + SHARES) % SHARES], share_sems.at[0, d])
    empty = jnp.zeros((width, LANES), BF16)
    for g in range(groups):
        first = pieces_before(g, per_chunk, chunks)
        level = g // per_chunk
        for c in range(chunks):
            n = first + c - level
            corr_ref[g * width : (g + 1) * width, c * LANES : (c + 1) * LANES] = (
                empty if c < level else blocks[n % SHARES, n // SHARES]
            )
    wait(xs.at[rest], recv_sems.at[2])
    low_rows = pairs * paths + half
    both = [xs[g].astype(F32) for g in range(groups)]
    lefts = jnp.concatenate([b[:, :width] for b in both], axis=1)
    rights = jnp.concatenate([b[:, width:] for b in both], axis=1)
    state = lefts[:paths]
    shocks = [rights[:paths]]
    for k in range(1, pairs):
        shocks.extend([lefts[k * paths : (k + 1) * paths], rights[k * paths : (k + 1) * paths]])
    shocks.append(
        jnp.concatenate([lefts[pairs * paths : low_rows], rights[pairs * paths : low_rows]], axis=0)
    )
    ones = jnp.ones((paths, PAD), BF16)
    for k in range(steps):
        states[k] = state
        u = jnp.tanh(state)
        source = alpha * (1.0 + tilt * u + curve * u * u) * shocks[k]
        state = damping * state + ROOT_STEP * split_mm(source, corr_ref[...], NN)
        high, low = split(state)
        for b in range(groups):
            cols = slice(b * width, (b + 1) * width)
            parts[b, k * paths : (k + 1) * paths, :] = jnp.concatenate(
                [high[:, cols], low[:, cols], ones], axis=1
            )

    exposure[...] = jnp.zeros_like(exposure)

    def trade_rows(s, b):
        code = trades[s, b, 2].astype(jnp.int32)
        return trades[s, b, 0], trades[s, b, 1], code & ((1 << bits) - 1), code >> bits

    def forward(s, slot, b, carry):
        notional, strike, in_set, factor = trade_rows(s, slot)
        table = one_hot(factor, width)
        high, low = split(-strike)
        tail = jnp.concatenate([high, low, jnp.zeros((PAD - 2, tile), BF16)], axis=0)
        money = mm(parts[b], jnp.concatenate([table, table, tail], axis=0), NN)
        squash = jnp.tanh(money).astype(BF16)
        squashes[s, b] = squash
        exposure[...] += mm(squash, one_hot(in_set, sets, notional), NT)
        return carry

    every = pl.ds(0, groups)
    wait(trades.at[share, rest], recv_sems.at[1])
    start_share(trades.at[share, every], 4)
    lax.fori_loop(0, SHARES, lambda s, c: forward(s, groups, me_f, c), 0, unroll=SHARES)

    def forward_share(d, carry):
        s = (share - d + SHARES) % SHARES

        @pl.when(d > 0)
        def _():
            wait(trades.at[s, every], share_sems.at[1, d])

        def forward_other(n, carry):
            b = (me_f + n) % groups
            return forward(s, b, b, carry)

        return lax.fori_loop(1, groups, forward_other, carry, unroll=groups - 1)

    lax.fori_loop(0, SHARES, forward_share, 0)

    for k in range(steps):
        at = slice(k * paths, (k + 1) * paths)
        scale = math.exp(-DISCOUNT_RATE * TIME_STEP * (k + 1)) * loss_ref[...]
        weights[at, :] = (scale * jax.nn.sigmoid(exposure[at, :])).astype(BF16)
    terms[...] = jnp.zeros_like(terms)

    def backward(i, carry):
        s, b = i % SHARES, i // SHARES
        notional, strike, in_set, factor = trade_rows(s, b)
        pulled = mm(weights[...], one_hot(in_set, sets), NN)
        squash = squashes[s, b].astype(F32)
        pulled = (pulled * (notional * (1.0 - squash * squash))).astype(BF16)
        terms[b] += mm(pulled, one_hot(factor, width), NT)
        return carry

    lax.fori_loop(0, SHARES * groups, backward, 0, unroll=UNROLL)

    adjoint = jnp.zeros((paths, factors), F32)
    sums = [jnp.zeros((1, factors), F32) for _ in range(3)]
    for k in reversed(range(steps)):
        adjoint = adjoint + jnp.concatenate(
            [terms[b, k * paths : (k + 1) * paths, :] for b in range(groups)], axis=1
        )
        u = jnp.tanh(states[k])
        vbar = split_mm(ROOT_STEP * adjoint, corr_ref[...], NT) * shocks[k]
        for at, slope in enumerate(
            (
                1.0 + tilt * u + curve * u * u,
                alpha * (0.5 * nu * u - 0.25 * rho * nu * nu * u * u),
                alpha * (0.5 * rho * u + curve2 * nu * u * u / 12.0),
            )
        ):
            sums[at] = sums[at] + jnp.sum(vbar * slope, axis=0, keepdims=True)
        adjoint = damping * adjoint + vbar * (alpha * (tilt + 2.0 * curve * u)) * (1.0 - u * u)

    for g in range(groups):
        cols = slice(g * width, (g + 1) * width)
        back_send[g] = jnp.concatenate([adjoint[:half, cols], adjoint[half:, cols]], axis=1).astype(BF16)

    for d in away:
        start(back_send.at[(me_f + d) % groups], back.at[me_f], 5, device_at(d))
    back[me_f] = back_send[me_f]
    stacked = jnp.concatenate(sums + [jnp.zeros((5, factors), F32)], axis=0)
    thirds = mm(jnp.concatenate(split3(stacked), axis=0), slice_table, NT)
    rows = thirds[0:8] + (thirds[8:16] + thirds[16:24])
    totals[me] = jnp.concatenate([rows[n : n + 1] for n in range(4)], axis=1)
    for at in others:
        start(totals.at[me], totals.at[me], 6, device_at(at))

    @pl.when(my_chunk < chunks)
    def _():
        for _ in away:
            wait(blocks.at[share, my_slot], send_sems.at[0])

    wait(trades.at[share, rest], send_sems.at[1])
    wait(xs.at[rest], send_sems.at[2])
    wait(par.at[rest], send_sems.at[7])
    for d in range(1, SHARES):
        wait(blocks.at[share], send_sems.at[3])
        wait(trades.at[share, every], send_sems.at[4])
    wait(back.at[rest], send_sems.at[5])
    wait(totals.at[pl.ds(0, len(others))], send_sems.at[6])
    wait(back.at[rest], recv_sems.at[5])
    wait(totals.at[pl.ds(0, len(others))], recv_sems.at[6])


def finish_kernel(back_ref, totals_ref, a_ref, g_ref):
    groups = back_ref.shape[0]
    width, path_cols = a_ref.shape
    slices = g_ref.shape[1]
    pieces = []
    for g in range(groups):
        piece = back_ref[g].astype(F32)
        pieces.extend([piece[:, :width], piece[:, width:]])
    a_ref[...] = jnp.concatenate(pieces, axis=0).T
    path_groups = totals_ref.shape[0] // groups
    total = jnp.sum(totals_ref[...], axis=0) / (path_cols * path_groups)
    g_ref[...] = jnp.concatenate([total[:, n * slices : (n + 1) * slices] for n in range(3)], axis=0)


def per_device(
    x_start,
    shocks,
    cholesky,
    reversion,
    sabr_alpha,
    sabr_rho,
    sabr_nu,
    factor_slice,
    notional,
    strike,
    trade_set,
    trade_factor,
    loss_given,
):
    width, path_cols = x_start.shape
    steps, factors = shocks.shape[0], cholesky.shape[0]
    groups = lax.axis_size("factors")
    path_groups = lax.axis_size("paths")
    devices = groups * path_groups
    paths = path_cols // groups
    trades_here = notional.shape[0]
    tile = trades_here // SHARES
    rows, sets, slices = steps * paths, loss_given.shape[0], sabr_alpha.shape[0]
    fold = LANES // width
    pairs = steps // 2
    path_rows = pairs * paths + paths // 2
    slots = pieces_before(groups, fold, factors // LANES) // SHARES
    vmem, dma = pltpu.VMEM, pltpu.SemaphoreType.DMA
    whole = pl.BlockSpec(memory_space=pltpu.VMEM)
    back, totals = pl.pallas_call(
        fused_kernel,
        out_shape=(
            jax.ShapeDtypeStruct((groups, paths // 2, 2 * width), BF16),
            jax.ShapeDtypeStruct((devices, 1, 4 * slices), F32),
        ),
        in_specs=[pl.BlockSpec(memory_space=pl.ANY)] * 13,
        out_specs=(whole,) * 2,
        scratch_shapes=[
            vmem((width, path_cols), F32),
            vmem((steps, width, path_cols), F32),
            vmem((width, factors), F32),
            vmem((1, width), F32),
            vmem((1, slices), F32),
            vmem((1, slices), F32),
            vmem((1, slices), F32),
            vmem((1, width), jnp.int32),
            vmem((1, trades_here), F32),
            vmem((1, trades_here), F32),
            vmem((1, trades_here), jnp.int32),
            vmem((1, trades_here), jnp.int32),
            vmem((1, sets), F32),
            vmem((groups, 1, 2 * width), F32),
            vmem((SHARES, slots, width, LANES), BF16),
            vmem((factors, factors), BF16),
            vmem((groups, path_rows, 2 * width), BF16),
            vmem((groups, path_rows, 2 * width), BF16),
            vmem((SHARES, groups + 1, 3, 1, tile), F32),
            vmem((steps, paths, factors), F32),
            vmem((groups, rows, 2 * width + PAD), BF16),
            vmem((SHARES, groups, rows, tile), BF16),
            vmem((rows, sets), F32),
            vmem((rows, sets), BF16),
            vmem((groups, rows, width), F32),
            vmem((groups, paths // 2, 2 * width), BF16),
            dma((13,)),
            dma((8,)),
            dma((8,)),
            dma((2, SHARES)),
        ],
        compiler_params=pltpu.CompilerParams(
            collective_id=0, has_side_effects=True, vmem_limit_bytes=56 * 1024 * 1024
        ),
    )(
        x_start,
        shocks,
        cholesky.T,
        reversion[None, :],
        sabr_alpha[None, :],
        sabr_rho[None, :],
        sabr_nu[None, :],
        factor_slice[None, :],
        notional[None, :],
        strike[None, :],
        trade_set[None, :],
        trade_factor[None, :],
        loss_given[None, :],
    )
    return pl.pallas_call(
        finish_kernel,
        out_shape=(
            jax.ShapeDtypeStruct((width, path_cols), F32),
            jax.ShapeDtypeStruct((3, slices), F32),
        ),
        in_specs=[whole] * 2,
        out_specs=(whole,) * 2,
    )(back, totals)


def solution(mesh):
    return jax.shard_map(
        per_device,
        mesh=mesh,
        in_specs=(
            P("factors", "paths"),
            P(None, "factors", "paths"),
            P(None, "factors"),
            P("factors"),
            P(),
            P(),
            P(),
            P("factors"),
            P("factors"),
            P("factors"),
            P("factors"),
            P("factors"),
            P(),
        ),
        out_specs=(P("factors", "paths"), P()),
        check_vma=False,
    )
```

```python
import functools
import math

import jax
import jax.numpy as jnp
from jax import lax
from jax.experimental import pallas as pl
from jax.experimental.pallas import tpu as pltpu
from jax.sharding import PartitionSpec as P

TIME_STEP = 0.25
ROOT_STEP = 0.5
DISCOUNT_RATE = 0.03
PRECISE = lax.Precision.HIGHEST
MESH = pl.DeviceIdType.MESH
NN = (((1,), (0,)), ((), ()))
NT = (((1,), (1,)), ((), ()))
F32 = jnp.float32
BF16 = jnp.bfloat16
SHARES = 4
PAD = 16
LANES = 128
UNROLL = 8


def mm(a, b, dims):
    return lax.dot_general(a, b, dims, preferred_element_type=F32)


def split(a):
    high = a.astype(BF16)
    return high, (a - high.astype(F32)).astype(BF16)


def split3(a):
    high, rest = a.astype(BF16), a - a.astype(BF16).astype(F32)
    return (high,) + split(rest)


def split_mm(a, b, dims):
    rows = a.shape[0]
    both = mm(jnp.concatenate(split(a), axis=0), b, dims)
    return both[:rows] + both[rows:]


def one_hot(ids, count, value=None):
    shape = (count, ids.shape[1])
    rows = lax.broadcasted_iota(jnp.int16, shape, 0)
    value = jnp.ones((1, 1), BF16) if value is None else value.astype(BF16)
    hit = rows == jnp.broadcast_to(ids.astype(jnp.int16), shape)
    return jnp.where(hit, jnp.broadcast_to(value, shape), jnp.zeros(shape, BF16))


def wrap(n, size):
    return jnp.where(n >= size, n - size, n)


def pieces_before(g, per_chunk, chunks):
    level = g // per_chunk
    return per_chunk * (chunks * level - level * (level - 1) // 2) + g % per_chunk * (chunks - level)


def fused_kernel(
    x_hbm,
    shocks_hbm,
    lt_hbm,
    reversion_hbm,
    alpha_hbm,
    rho_hbm,
    nu_hbm,
    slice_hbm,
    notional_hbm,
    strike_hbm,
    set_hbm,
    factor_hbm,
    loss_hbm,
    back,
    totals,
    x_ref,
    shocks_ref,
    lt_ref,
    reversion_ref,
    alpha_ref,
    rho_ref,
    nu_ref,
    slice_ref,
    notional_ref,
    strike_ref,
    set_ref,
    factor_ref,
    loss_ref,
    par,
    blocks,
    corr_ref,
    xs_send,
    xs,
    trades,
    states,
    parts,
    squashes,
    exposure,
    weights,
    terms,
    back_send,
    load,
    send_sems,
    recv_sems,
    share_sems,
):
    steps, width, path_cols = shocks_ref.shape
    groups = xs.shape[0]
    factors = corr_ref.shape[0]
    paths = path_cols // groups
    devices = totals.shape[0]
    path_groups = devices // groups
    sets = loss_ref.shape[1]
    slices = alpha_ref.shape[1]
    tile = trades.shape[4]
    pairs = steps // 2
    half = paths // 2
    slots = blocks.shape[1]
    bits = (sets - 1).bit_length()
    chunks = factors // LANES
    per_chunk = LANES // width

    me_f = lax.axis_index("factors")
    me_p = lax.axis_index("paths")
    share = me_p % SHARES
    share_base = me_p - share
    me = me_p * groups + me_f

    pairs_in = [
        (lt_hbm, lt_ref),
        (reversion_hbm, reversion_ref),
        (slice_hbm, slice_ref),
        (x_hbm, x_ref),
        (shocks_hbm, shocks_ref),
        (notional_hbm, notional_ref),
        (strike_hbm, strike_ref),
        (set_hbm, set_ref),
        (factor_hbm, factor_ref),
        (alpha_hbm, alpha_ref),
        (rho_hbm, rho_ref),
        (nu_hbm, nu_ref),
        (loss_hbm, loss_ref),
    ]
    loads = [
        pltpu.make_async_copy(src, dst, load.at[n]) for n, (src, dst) in enumerate(pairs_in)
    ]

    def loaded(*which):
        for n in which:
            loads[n].wait()

    loads[0].start()

    def device_at(d):
        if isinstance(d, tuple):
            return {"paths": wrap(me_p + d[0], path_groups), "factors": wrap(me_f + d[1], groups)}
        return {"factors": wrap(me_f + d, groups)}

    others = [(e, d) for e in range(path_groups) for d in range(groups) if e + d]
    barrier = pltpu.get_barrier_semaphore()
    near = [(e, d) for e, d in others if e == 0 or d == 0]
    for at in near:
        pl.semaphore_signal(barrier, inc=1, device_id=device_at(at), device_id_type=MESH)
    for copy in loads[1:]:
        copy.start()

    def owned(g):
        level = g // per_chunk
        before = pieces_before(g, per_chunk, chunks)
        step = (share - before % SHARES + SHARES) % SHARES
        return level + step, (before + step) // SHARES

    my_chunk, my_slot = owned(me_f)
    my_cols = pl.ds(pl.multiple_of(my_chunk % chunks * LANES, LANES), LANES)
    loaded(0)

    @pl.when(my_chunk < chunks)
    def _():
        blocks[share, my_slot] = lt_ref[:, my_cols].astype(BF16)

    loaded(1, 2)
    par[me_f] = jnp.concatenate([reversion_ref[...], slice_ref[...].astype(F32)], axis=1)
    pl.semaphore_wait(barrier, len(near))

    def start(src, dst, kind, peer):
        pltpu.make_async_remote_copy(
            src_ref=src,
            dst_ref=dst,
            send_sem=send_sems.at[kind],
            recv_sem=recv_sems.at[kind],
            device_id=peer,
            device_id_type=MESH,
        ).start()

    def wait(ref, sem):
        pltpu.make_async_copy(ref, ref, sem).wait()

    away = range(1, groups)
    rest = pl.ds(0, groups - 1)

    @pl.when(my_chunk < chunks)
    def _():
        for d in away:
            start(blocks.at[share, my_slot], blocks.at[share, my_slot], 0, device_at(d))

    for d in away:
        start(par.at[me_f], par.at[me_f], 7, device_at(d))
    loaded(3, 4)
    columns = [jnp.concatenate([x_ref[...], shocks_ref[0]], axis=0).astype(BF16).T]
    for k in range(1, pairs):
        pair = jnp.concatenate([shocks_ref[2 * k - 1], shocks_ref[2 * k]], axis=0)
        columns.append(pair.astype(BF16).T)
    final = shocks_ref[steps - 1].astype(BF16).T
    for g in range(groups):
        top = g * paths
        for k in range(pairs):
            xs_send[g, k * paths : (k + 1) * paths] = columns[k][top : top + paths]
        xs_send[g, pairs * paths :] = jnp.concatenate(
            [final[top : top + half], final[top + half : top + paths]], axis=1
        )
    xs[me_f] = xs_send[me_f]
    for d in away:
        start(xs_send.at[wrap(me_f + d, groups)], xs.at[me_f], 2, device_at(d))

    loaded(5, 6, 7, 8)
    for n in range(SHARES):
        cols = slice(n * tile, (n + 1) * tile)
        code = set_ref[:, cols] + ((factor_ref[:, cols] - me_f * width) << bits)
        trades[n, groups, 0] = notional_ref[:, cols]
        trades[n, groups, 1] = strike_ref[:, cols]
        trades[n, groups, 2] = code.astype(F32)
    trades[share, me_f] = trades[share, groups]
    for d in away:
        start(trades.at[share, me_f], trades.at[share, me_f], 1, device_at(d))

    @pl.when(my_chunk < chunks)
    def _():
        wait(blocks.at[share, pl.ds(0, slots - 1)], recv_sems.at[0])

    @pl.when(my_chunk >= chunks)
    def _():
        wait(blocks.at[share], recv_sems.at[0])

    def paired(d):
        if d == 2:
            return wrap(share + 2, SHARES)
        return share + 1 - 2 * (share % 2) if d == 1 else SHARES - 1 - share

    def start_share(ref, kind):
        for d in (2, 3, 1):
            peer = {"paths": share_base + paired(d)}
            pltpu.make_async_remote_copy(
                src_ref=ref,
                dst_ref=ref,
                send_sem=send_sems.at[kind],
                recv_sem=share_sems.at[kind - 3, d],
                device_id=peer,
                device_id_type=MESH,
            ).start()

    start_share(blocks.at[share], 3)
    loaded(9, 10, 11, 12)
    wait(par.at[rest], recv_sems.at[7])
    all_par = [par[g] for g in range(groups)]
    damping = 1.0 - jnp.concatenate([p[:, :width] for p in all_par], axis=1) * TIME_STEP
    slice_ids = jnp.concatenate([p[:, width:] for p in all_par], axis=1)
    slice_rows = lax.broadcasted_iota(jnp.int32, (slices, factors), 0).astype(F32)
    slice_table = jnp.where(slice_rows == slice_ids, 1.0, 0.0).astype(BF16)
    smile = jnp.concatenate(
        [alpha_ref[...], rho_ref[...], nu_ref[...], jnp.zeros((5, slices), F32)], axis=0
    )
    smile = mm(jnp.concatenate(split3(smile), axis=0), slice_table, NN)
    smile = smile[0:8] + (smile[8:16] + smile[16:24])
    alpha, rho, nu = smile[0:1, :], smile[1:2, :], smile[2:3, :]
    curve2 = 2.0 - 3.0 * rho * rho
    curve = curve2 * nu * nu / 24.0
    tilt = 0.5 * rho * nu

    for d in range(1, SHARES):
        wait(blocks.at[paired(d)], share_sems.at[0, d])
    empty = jnp.zeros((width, LANES), BF16)
    for g in range(groups):
        first = pieces_before(g, per_chunk, chunks)
        level = g // per_chunk
        for c in range(chunks):
            n = first + c - level
            corr_ref[g * width : (g + 1) * width, c * LANES : (c + 1) * LANES] = (
                empty if c < level else blocks[n % SHARES, n // SHARES]
            )
    wait(xs.at[rest], recv_sems.at[2])
    low_rows = pairs * paths + half
    both = [xs[g].astype(F32) for g in range(groups)]
    lefts = jnp.concatenate([b[:, :width] for b in both], axis=1)
    rights = jnp.concatenate([b[:, width:] for b in both], axis=1)
    state = lefts[:paths]
    shocks = [rights[:paths]]
    for k in range(1, pairs):
        shocks.extend([lefts[k * paths : (k + 1) * paths], rights[k * paths : (k + 1) * paths]])
    shocks.append(
        jnp.concatenate([lefts[pairs * paths : low_rows], rights[pairs * paths : low_rows]], axis=0)
    )
    ones = jnp.ones((paths, PAD), BF16)
    for k in range(steps):
        states[k] = state
        u = jnp.tanh(state)
        source = alpha * (1.0 + tilt * u + curve * u * u) * shocks[k]
        state = damping * state + ROOT_STEP * split_mm(source, corr_ref[...], NN)
        high, low = split(state)
        for b in range(groups):
            cols = slice(b * width, (b + 1) * width)
            parts[b, k * paths : (k + 1) * paths, :] = jnp.concatenate(
                [high[:, cols], low[:, cols], ones], axis=1
            )

    exposure[...] = jnp.zeros_like(exposure)

    def trade_rows(s, b):
        code = trades[s, b, 2].astype(jnp.int32)
        return trades[s, b, 0], trades[s, b, 1], code & ((1 << bits) - 1), code >> bits

    def forward(s, slot, b=None):
        b = slot if b is None else b
        notional, strike, in_set, factor = trade_rows(s, slot)
        table = one_hot(factor, width)
        high, low = split(-strike)
        tail = jnp.concatenate([high, low, jnp.zeros((PAD - 2, tile), BF16)], axis=0)
        money = mm(parts[b], jnp.concatenate([table, table, tail], axis=0), NN)
        squash = jnp.tanh(money).astype(BF16)
        squashes[s, b] = squash
        exposure[...] += mm(squash, one_hot(in_set, sets, notional), NT)

    every = pl.ds(0, groups)
    wait(trades.at[share, rest], recv_sems.at[1])
    start_share(trades.at[share, every], 4)
    for n in range(SHARES):
        forward(n, groups, me_f)
    for n in away:
        forward(share, wrap(me_f + n, groups))
    wait(trades.at[paired(1), every], share_sems.at[1, 1])
    for n in away:
        forward(paired(1), wrap(me_f + n, groups))
    for d in (2, 3):
        wait(trades.at[paired(d), every], share_sems.at[1, d])
    for n in away:
        for d in (2, 3):
            forward(paired(d), wrap(me_f + n, groups))

    for k in range(steps):
        at = slice(k * paths, (k + 1) * paths)
        scale = math.exp(-DISCOUNT_RATE * TIME_STEP * (k + 1)) * loss_ref[...]
        weights[at, :] = (scale * jax.nn.sigmoid(exposure[at, :])).astype(BF16)
    terms[...] = jnp.zeros_like(terms)

    def backward(i, carry):
        s, b = i % SHARES, i // SHARES
        notional, strike, in_set, factor = trade_rows(s, b)
        pulled = mm(weights[...], one_hot(in_set, sets), NN)
        squash = squashes[s, b].astype(F32)
        pulled = (pulled * (notional * (1.0 - squash * squash))).astype(BF16)
        terms[b] += mm(pulled, one_hot(factor, width), NT)
        return carry

    lax.fori_loop(0, SHARES * groups, backward, 0, unroll=UNROLL)

    adjoint = jnp.zeros((paths, factors), F32)
    sums = [jnp.zeros((1, factors), F32) for _ in range(3)]
    for k in reversed(range(steps)):
        adjoint = adjoint + jnp.concatenate(
            [terms[b, k * paths : (k + 1) * paths, :] for b in range(groups)], axis=1
        )
        u = jnp.tanh(states[k])
        vbar = split_mm(ROOT_STEP * adjoint, corr_ref[...], NT) * shocks[k]
        for at, slope in enumerate(
            (
                1.0 + tilt * u + curve * u * u,
                alpha * (0.5 * nu * u - 0.25 * rho * nu * nu * u * u),
                alpha * (0.5 * rho * u + curve2 * nu * u * u / 12.0),
            )
        ):
            sums[at] = sums[at] + jnp.sum(vbar * slope, axis=0, keepdims=True)
        adjoint = damping * adjoint + vbar * (alpha * (tilt + 2.0 * curve * u)) * (1.0 - u * u)

    for g in range(groups):
        cols = slice(g * width, (g + 1) * width)
        back_send[g] = jnp.concatenate([adjoint[:half, cols], adjoint[half:, cols]], axis=1).astype(BF16)

    for d in away:
        start(back_send.at[wrap(me_f + d, groups)], back.at[me_f], 5, device_at(d))
    back[me_f] = back_send[me_f]
    stacked = jnp.concatenate(sums + [jnp.zeros((5, factors), F32)], axis=0)
    thirds = mm(jnp.concatenate(split3(stacked), axis=0), slice_table, NT)
    rows = thirds[0:8] + (thirds[8:16] + thirds[16:24])
    totals[me] = jnp.concatenate([rows[n : n + 1] for n in range(4)], axis=1)
    for at in others:
        start(totals.at[me], totals.at[me], 6, device_at(at))

    @pl.when(my_chunk < chunks)
    def _():
        for _ in away:
            wait(blocks.at[share, my_slot], send_sems.at[0])

    wait(trades.at[share, rest], send_sems.at[1])
    wait(xs.at[rest], send_sems.at[2])
    wait(par.at[rest], send_sems.at[7])
    for d in range(1, SHARES):
        wait(blocks.at[share], send_sems.at[3])
        wait(trades.at[share, every], send_sems.at[4])
    wait(back.at[rest], send_sems.at[5])
    wait(totals.at[pl.ds(0, len(others))], send_sems.at[6])
    wait(back.at[rest], recv_sems.at[5])
    wait(totals.at[pl.ds(0, len(others))], recv_sems.at[6])


def finish_kernel(back_ref, totals_ref, a_ref, g_ref):
    groups = back_ref.shape[0]
    width, path_cols = a_ref.shape
    slices = g_ref.shape[1]
    pieces = []
    for g in range(groups):
        piece = back_ref[g].astype(F32)
        pieces.extend([piece[:, :width], piece[:, width:]])
    a_ref[...] = jnp.concatenate(pieces, axis=0).T
    path_groups = totals_ref.shape[0] // groups
    total = jnp.sum(totals_ref[...], axis=0) / (path_cols * path_groups)
    g_ref[...] = jnp.concatenate([total[:, n * slices : (n + 1) * slices] for n in range(3)], axis=0)


def per_device(
    x_start,
    shocks,
    cholesky,
    reversion,
    sabr_alpha,
    sabr_rho,
    sabr_nu,
    factor_slice,
    notional,
    strike,
    trade_set,
    trade_factor,
    loss_given,
):
    width, path_cols = x_start.shape
    steps, factors = shocks.shape[0], cholesky.shape[0]
    groups = lax.axis_size("factors")
    path_groups = lax.axis_size("paths")
    devices = groups * path_groups
    paths = path_cols // groups
    trades_here = notional.shape[0]
    tile = trades_here // SHARES
    rows, sets, slices = steps * paths, loss_given.shape[0], sabr_alpha.shape[0]
    fold = LANES // width
    pairs = steps // 2
    path_rows = pairs * paths + paths // 2
    slots = pieces_before(groups, fold, factors // LANES) // SHARES
    vmem, dma = pltpu.VMEM, pltpu.SemaphoreType.DMA
    whole = pl.BlockSpec(memory_space=pltpu.VMEM)
    back, totals = pl.pallas_call(
        fused_kernel,
        out_shape=(
            jax.ShapeDtypeStruct((groups, paths // 2, 2 * width), BF16),
            jax.ShapeDtypeStruct((devices, 1, 4 * slices), F32),
        ),
        in_specs=[pl.BlockSpec(memory_space=pl.ANY)] * 13,
        out_specs=(whole,) * 2,
        scratch_shapes=[
            vmem((width, path_cols), F32),
            vmem((steps, width, path_cols), F32),
            vmem((width, factors), F32),
            vmem((1, width), F32),
            vmem((1, slices), F32),
            vmem((1, slices), F32),
            vmem((1, slices), F32),
            vmem((1, width), jnp.int32),
            vmem((1, trades_here), F32),
            vmem((1, trades_here), F32),
            vmem((1, trades_here), jnp.int32),
            vmem((1, trades_here), jnp.int32),
            vmem((1, sets), F32),
            vmem((groups, 1, 2 * width), F32),
            vmem((SHARES, slots, width, LANES), BF16),
            vmem((factors, factors), BF16),
            vmem((groups, path_rows, 2 * width), BF16),
            vmem((groups, path_rows, 2 * width), BF16),
            vmem((SHARES, groups + 1, 3, 1, tile), F32),
            vmem((steps, paths, factors), F32),
            vmem((groups, rows, 2 * width + PAD), BF16),
            vmem((SHARES, groups, rows, tile), BF16),
            vmem((rows, sets), F32),
            vmem((rows, sets), BF16),
            vmem((groups, rows, width), F32),
            vmem((groups, paths // 2, 2 * width), BF16),
            dma((13,)),
            dma((8,)),
            dma((8,)),
            dma((2, SHARES)),
        ],
        compiler_params=pltpu.CompilerParams(
            collective_id=0, has_side_effects=True, vmem_limit_bytes=56 * 1024 * 1024
        ),
    )(
        x_start,
        shocks,
        cholesky.T,
        reversion[None, :],
        sabr_alpha[None, :],
        sabr_rho[None, :],
        sabr_nu[None, :],
        factor_slice[None, :],
        notional[None, :],
        strike[None, :],
        trade_set[None, :],
        trade_factor[None, :],
        loss_given[None, :],
    )
    return pl.pallas_call(
        finish_kernel,
        out_shape=(
            jax.ShapeDtypeStruct((width, path_cols), F32),
            jax.ShapeDtypeStruct((3, slices), F32),
        ),
        in_specs=[whole] * 2,
        out_specs=(whole,) * 2,
    )(back, totals)


def solution(mesh):
    return jax.shard_map(
        per_device,
        mesh=mesh,
        in_specs=(
            P("factors", "paths"),
            P(None, "factors", "paths"),
            P(None, "factors"),
            P("factors"),
            P(),
            P(),
            P(),
            P("factors"),
            P("factors"),
            P("factors"),
            P("factors"),
            P("factors"),
            P(),
        ),
        out_specs=(P("factors", "paths"), P()),
        check_vma=False,
    )
```

```python
import functools
import math

import jax
import jax.numpy as jnp
from jax import lax
from jax.experimental import pallas as pl
from jax.experimental.pallas import tpu as pltpu
from jax.sharding import PartitionSpec as P

TIME_STEP = 0.25
ROOT_STEP = 0.5
DISCOUNT_RATE = 0.03
PRECISE = lax.Precision.HIGHEST
MESH = pl.DeviceIdType.MESH
NN = (((1,), (0,)), ((), ()))
NT = (((1,), (1,)), ((), ()))
F32 = jnp.float32
BF16 = jnp.bfloat16
SHARES = 4
PAD = 16
LANES = 128
RUN = 2


def mm(a, b, dims):
    return lax.dot_general(a, b, dims, preferred_element_type=F32)


def split(a):
    high = a.astype(BF16)
    return high, (a - high.astype(F32)).astype(BF16)


def split3(a):
    high, rest = a.astype(BF16), a - a.astype(BF16).astype(F32)
    return (high,) + split(rest)


def split_mm(a, b, dims):
    rows = a.shape[0]
    both = mm(jnp.concatenate(split(a), axis=0), b, dims)
    return both[:rows] + both[rows:]


def one_hot(ids, count, value=None):
    shape = (count, ids.shape[1])
    rows = lax.broadcasted_iota(jnp.int16, shape, 0)
    value = jnp.ones((1, 1), BF16) if value is None else value.astype(BF16)
    hit = rows == jnp.broadcast_to(ids.astype(jnp.int16), shape)
    return jnp.where(hit, jnp.broadcast_to(value, shape), jnp.zeros(shape, BF16))


def wrap(n, size):
    return jnp.where(n >= size, n - size, n)


def pieces_before(g, per_chunk, chunks):
    level = g // per_chunk
    return per_chunk * (chunks * level - level * (level - 1) // 2) + g % per_chunk * (chunks - level)


def fused_kernel(
    x_hbm,
    shocks_hbm,
    lt_hbm,
    reversion_hbm,
    alpha_hbm,
    rho_hbm,
    nu_hbm,
    slice_hbm,
    notional_hbm,
    strike_hbm,
    set_hbm,
    factor_hbm,
    loss_hbm,
    back,
    totals,
    x_ref,
    shocks_ref,
    lt_ref,
    reversion_ref,
    alpha_ref,
    rho_ref,
    nu_ref,
    slice_ref,
    notional_ref,
    strike_ref,
    set_ref,
    factor_ref,
    loss_ref,
    par,
    blocks,
    corr_ref,
    xs_send,
    xs,
    trades,
    states,
    parts,
    squashes,
    exposure,
    weights,
    terms,
    back_send,
    load,
    send_sems,
    recv_sems,
    share_sems,
):
    steps, width, path_cols = shocks_ref.shape
    groups = xs.shape[0]
    factors = corr_ref.shape[0]
    paths = path_cols // groups
    devices = totals.shape[0]
    path_groups = devices // groups
    sets = loss_ref.shape[1]
    slices = alpha_ref.shape[1]
    tile = trades.shape[4]
    pairs = steps // 2
    half = paths // 2
    slots = blocks.shape[1]
    bits = (sets - 1).bit_length()
    chunks = factors // LANES
    per_chunk = LANES // width

    me_f = lax.axis_index("factors")
    me_p = lax.axis_index("paths")
    share = me_p % SHARES
    share_base = me_p - share
    me = me_p * groups + me_f

    pairs_in = [
        (lt_hbm, lt_ref),
        (reversion_hbm, reversion_ref),
        (slice_hbm, slice_ref),
        (x_hbm, x_ref),
        (shocks_hbm, shocks_ref),
        (notional_hbm, notional_ref),
        (strike_hbm, strike_ref),
        (set_hbm, set_ref),
        (factor_hbm, factor_ref),
        (alpha_hbm, alpha_ref),
        (rho_hbm, rho_ref),
        (nu_hbm, nu_ref),
        (loss_hbm, loss_ref),
    ]
    loads = [
        pltpu.make_async_copy(src, dst, load.at[n]) for n, (src, dst) in enumerate(pairs_in)
    ]

    def loaded(*which):
        for n in which:
            loads[n].wait()

    loads[0].start()

    def device_at(d):
        if isinstance(d, tuple):
            return {"paths": wrap(me_p + d[0], path_groups), "factors": wrap(me_f + d[1], groups)}
        return {"factors": wrap(me_f + d, groups)}

    others = [(e, d) for e in range(path_groups) for d in range(groups) if e + d]
    barrier = pltpu.get_barrier_semaphore()
    near = [(e, d) for e, d in others if e == 0 or d == 0]
    for at in near:
        pl.semaphore_signal(barrier, inc=1, device_id=device_at(at), device_id_type=MESH)
    for copy in loads[1:]:
        copy.start()

    def owned(g):
        level = g // per_chunk
        before = pieces_before(g, per_chunk, chunks)
        step = (share - before % SHARES + SHARES) % SHARES
        return level + step, (before + step) // SHARES

    my_chunk, my_slot = owned(me_f)
    my_cols = pl.ds(pl.multiple_of(my_chunk % chunks * LANES, LANES), LANES)
    loaded(0)

    @pl.when(my_chunk < chunks)
    def _():
        blocks[share, my_slot] = lt_ref[:, my_cols].astype(BF16)

    loaded(1, 2)
    par[me_f] = jnp.concatenate([reversion_ref[...], slice_ref[...].astype(F32)], axis=1)
    pl.semaphore_wait(barrier, len(near))

    def start(src, dst, kind, peer):
        pltpu.make_async_remote_copy(
            src_ref=src,
            dst_ref=dst,
            send_sem=send_sems.at[kind],
            recv_sem=recv_sems.at[kind],
            device_id=peer,
            device_id_type=MESH,
        ).start()

    def wait(ref, sem):
        pltpu.make_async_copy(ref, ref, sem).wait()

    away = range(1, groups)
    rest = pl.ds(0, groups - 1)

    @pl.when(my_chunk < chunks)
    def _():
        for d in away:
            start(blocks.at[share, my_slot], blocks.at[share, my_slot], 0, device_at(d))

    for d in away:
        start(par.at[me_f], par.at[me_f], 7, device_at(d))
    loaded(3, 4)
    columns = [jnp.concatenate([x_ref[...], shocks_ref[0]], axis=0).astype(BF16).T]
    for k in range(1, pairs):
        pair = jnp.concatenate([shocks_ref[2 * k - 1], shocks_ref[2 * k]], axis=0)
        columns.append(pair.astype(BF16).T)
    final = shocks_ref[steps - 1].astype(BF16).T
    for g in range(groups):
        top = g * paths
        for k in range(pairs):
            xs_send[g, k * paths : (k + 1) * paths] = columns[k][top : top + paths]
        xs_send[g, pairs * paths :] = jnp.concatenate(
            [final[top : top + half], final[top + half : top + paths]], axis=1
        )
    xs[me_f] = xs_send[me_f]
    for d in away:
        start(xs_send.at[wrap(me_f + d, groups)], xs.at[me_f], 2, device_at(d))

    loaded(5, 6, 7, 8)
    for n in range(SHARES):
        cols = slice(n * tile, (n + 1) * tile)
        code = set_ref[:, cols] + ((factor_ref[:, cols] - me_f * width) << bits)
        trades[n, groups, 0] = notional_ref[:, cols]
        trades[n, groups, 1] = strike_ref[:, cols]
        trades[n, groups, 2] = code.astype(F32)
    trades[share, me_f] = trades[share, groups]
    for d in away:
        start(trades.at[share, me_f], trades.at[share, me_f], 1, device_at(d))

    @pl.when(my_chunk < chunks)
    def _():
        wait(blocks.at[share, pl.ds(0, slots - 1)], recv_sems.at[0])

    @pl.when(my_chunk >= chunks)
    def _():
        wait(blocks.at[share], recv_sems.at[0])

    def paired(d):
        if d == 2:
            return wrap(share + 2, SHARES)
        return share + 1 - 2 * (share % 2) if d == 1 else SHARES - 1 - share

    def start_share(ref, kind):
        for d in (2, 3, 1):
            peer = {"paths": share_base + paired(d)}
            pltpu.make_async_remote_copy(
                src_ref=ref,
                dst_ref=ref,
                send_sem=send_sems.at[kind],
                recv_sem=share_sems.at[kind - 3, d],
                device_id=peer,
                device_id_type=MESH,
            ).start()

    start_share(blocks.at[share], 3)
    loaded(9, 10, 11, 12)
    wait(par.at[rest], recv_sems.at[7])
    all_par = [par[g] for g in range(groups)]
    damping = 1.0 - jnp.concatenate([p[:, :width] for p in all_par], axis=1) * TIME_STEP
    slice_ids = jnp.concatenate([p[:, width:] for p in all_par], axis=1)
    slice_rows = lax.broadcasted_iota(jnp.int32, (slices, factors), 0).astype(F32)
    slice_table = jnp.where(slice_rows == slice_ids, 1.0, 0.0).astype(BF16)
    smile = jnp.concatenate(
        [alpha_ref[...], rho_ref[...], nu_ref[...], jnp.zeros((5, slices), F32)], axis=0
    )
    smile = mm(jnp.concatenate(split3(smile), axis=0), slice_table, NN)
    smile = smile[0:8] + (smile[8:16] + smile[16:24])
    alpha, rho, nu = smile[0:1, :], smile[1:2, :], smile[2:3, :]
    curve2 = 2.0 - 3.0 * rho * rho
    curve = curve2 * nu * nu / 24.0
    tilt = 0.5 * rho * nu

    for d in range(1, SHARES):
        wait(blocks.at[paired(d)], share_sems.at[0, d])
    empty = jnp.zeros((width, LANES), BF16)
    for g in range(groups):
        first = pieces_before(g, per_chunk, chunks)
        level = g // per_chunk
        for c in range(chunks):
            n = first + c - level
            corr_ref[g * width : (g + 1) * width, c * LANES : (c + 1) * LANES] = (
                empty if c < level else blocks[n % SHARES, n // SHARES]
            )
    wait(xs.at[rest], recv_sems.at[2])
    low_rows = pairs * paths + half
    both = [xs[g].astype(F32) for g in range(groups)]
    lefts = jnp.concatenate([b[:, :width] for b in both], axis=1)
    rights = jnp.concatenate([b[:, width:] for b in both], axis=1)
    state = lefts[:paths]
    shocks = [rights[:paths]]
    for k in range(1, pairs):
        shocks.extend([lefts[k * paths : (k + 1) * paths], rights[k * paths : (k + 1) * paths]])
    shocks.append(
        jnp.concatenate([lefts[pairs * paths : low_rows], rights[pairs * paths : low_rows]], axis=0)
    )
    ones = jnp.ones((paths, PAD), BF16)
    for k in range(steps):
        states[k] = state
        u = jnp.tanh(state)
        source = alpha * (1.0 + tilt * u + curve * u * u) * shocks[k]
        state = damping * state + ROOT_STEP * split_mm(source, corr_ref[...], NN)
        high, low = split(state)
        for b in range(groups):
            cols = slice(b * width, (b + 1) * width)
            parts[b, k * paths : (k + 1) * paths, :] = jnp.concatenate(
                [high[:, cols], low[:, cols], ones], axis=1
            )

    exposure[...] = jnp.zeros_like(exposure)

    def trade_rows(s, b):
        code = trades[s, b, 2].astype(jnp.int32)
        return trades[s, b, 0], trades[s, b, 1], code & ((1 << bits) - 1), code >> bits

    def forward(s, slot, b=None):
        b = slot if b is None else b
        notional, strike, in_set, factor = trade_rows(s, slot)
        table = one_hot(factor, width)
        high, low = split(-strike)
        tail = jnp.concatenate([high, low, jnp.zeros((PAD - 2, tile), BF16)], axis=0)
        money = mm(parts[b], jnp.concatenate([table, table, tail], axis=0), NN)
        squash = jnp.tanh(money).astype(BF16)
        squashes[s, b] = squash
        exposure[...] += mm(squash, one_hot(in_set, sets, notional), NT)

    every = pl.ds(0, groups)
    wait(trades.at[share, rest], recv_sems.at[1])
    start_share(trades.at[share, every], 4)
    for n in range(SHARES):
        forward(n, groups, me_f)
    for n in away:
        forward(share, wrap(me_f + n, groups))
    wait(trades.at[paired(1), every], share_sems.at[1, 1])
    for n in away:
        forward(paired(1), wrap(me_f + n, groups))
    for d in (2, 3):
        wait(trades.at[paired(d), every], share_sems.at[1, d])
    for n in away:
        for d in (2, 3):
            forward(paired(d), wrap(me_f + n, groups))

    for k in range(steps):
        at = slice(k * paths, (k + 1) * paths)
        scale = math.exp(-DISCOUNT_RATE * TIME_STEP * (k + 1)) * loss_ref[...]
        weights[at, :] = (scale * jax.nn.sigmoid(exposure[at, :])).astype(BF16)

    def backward(s, b):
        notional, strike, in_set, factor = trade_rows(s, b)
        pulled = mm(weights[...], one_hot(in_set, sets), NN)
        squash = squashes[s, b].astype(F32)
        pulled = (pulled * (notional * (1.0 - squash * squash))).astype(BF16)
        return mm(pulled, one_hot(factor, width), NT)

    for first in range(0, groups, RUN):

        @pl.when(me_f >= 0)
        def _():
            for b in range(first, first + RUN):
                for s in range(SHARES):
                    got = backward(s, b)
                    terms[b] = got if s == 0 else terms[b] + got


    adjoint = jnp.zeros((paths, factors), F32)
    sums = [jnp.zeros((1, factors), F32) for _ in range(3)]
    for k in reversed(range(steps)):
        adjoint = adjoint + jnp.concatenate(
            [terms[b, k * paths : (k + 1) * paths, :] for b in range(groups)], axis=1
        )
        u = jnp.tanh(states[k])
        vbar = split_mm(ROOT_STEP * adjoint, corr_ref[...], NT) * shocks[k]
        for at, slope in enumerate(
            (
                1.0 + tilt * u + curve * u * u,
                alpha * (0.5 * nu * u - 0.25 * rho * nu * nu * u * u),
                alpha * (0.5 * rho * u + curve2 * nu * u * u / 12.0),
            )
        ):
            sums[at] = sums[at] + jnp.sum(vbar * slope, axis=0, keepdims=True)
        adjoint = damping * adjoint + vbar * (alpha * (tilt + 2.0 * curve * u)) * (1.0 - u * u)

    for g in range(groups):
        cols = slice(g * width, (g + 1) * width)
        back_send[g] = jnp.concatenate([adjoint[:half, cols], adjoint[half:, cols]], axis=1).astype(BF16)

    for d in away:
        start(back_send.at[wrap(me_f + d, groups)], back.at[me_f], 5, device_at(d))
    back[me_f] = back_send[me_f]
    stacked = jnp.concatenate(sums + [jnp.zeros((5, factors), F32)], axis=0)
    thirds = mm(jnp.concatenate(split3(stacked), axis=0), slice_table, NT)
    rows = thirds[0:8] + (thirds[8:16] + thirds[16:24])
    totals[me] = jnp.concatenate([rows[n : n + 1] for n in range(4)], axis=1)
    for at in others:
        start(totals.at[me], totals.at[me], 6, device_at(at))

    @pl.when(my_chunk < chunks)
    def _():
        for _ in away:
            wait(blocks.at[share, my_slot], send_sems.at[0])

    wait(trades.at[share, rest], send_sems.at[1])
    wait(xs.at[rest], send_sems.at[2])
    wait(par.at[rest], send_sems.at[7])
    for d in range(1, SHARES):
        wait(blocks.at[share], send_sems.at[3])
        wait(trades.at[share, every], send_sems.at[4])
    wait(back.at[rest], send_sems.at[5])
    wait(totals.at[pl.ds(0, len(others))], send_sems.at[6])
    wait(back.at[rest], recv_sems.at[5])
    wait(totals.at[pl.ds(0, len(others))], recv_sems.at[6])


def finish_kernel(back_ref, totals_ref, a_ref, g_ref):
    groups = back_ref.shape[0]
    width, path_cols = a_ref.shape
    slices = g_ref.shape[1]
    pieces = []
    for g in range(groups):
        piece = back_ref[g].astype(F32)
        pieces.extend([piece[:, :width], piece[:, width:]])
    a_ref[...] = jnp.concatenate(pieces, axis=0).T
    path_groups = totals_ref.shape[0] // groups
    total = jnp.sum(totals_ref[...], axis=0) / (path_cols * path_groups)
    g_ref[...] = jnp.concatenate([total[:, n * slices : (n + 1) * slices] for n in range(3)], axis=0)


def per_device(
    x_start,
    shocks,
    cholesky,
    reversion,
    sabr_alpha,
    sabr_rho,
    sabr_nu,
    factor_slice,
    notional,
    strike,
    trade_set,
    trade_factor,
    loss_given,
):
    width, path_cols = x_start.shape
    steps, factors = shocks.shape[0], cholesky.shape[0]
    groups = lax.axis_size("factors")
    path_groups = lax.axis_size("paths")
    devices = groups * path_groups
    paths = path_cols // groups
    trades_here = notional.shape[0]
    tile = trades_here // SHARES
    rows, sets, slices = steps * paths, loss_given.shape[0], sabr_alpha.shape[0]
    fold = LANES // width
    pairs = steps // 2
    path_rows = pairs * paths + paths // 2
    slots = pieces_before(groups, fold, factors // LANES) // SHARES
    vmem, dma = pltpu.VMEM, pltpu.SemaphoreType.DMA
    whole = pl.BlockSpec(memory_space=pltpu.VMEM)
    back, totals = pl.pallas_call(
        fused_kernel,
        out_shape=(
            jax.ShapeDtypeStruct((groups, paths // 2, 2 * width), BF16),
            jax.ShapeDtypeStruct((devices, 1, 4 * slices), F32),
        ),
        in_specs=[pl.BlockSpec(memory_space=pl.ANY)] * 13,
        out_specs=(whole,) * 2,
        scratch_shapes=[
            vmem((width, path_cols), F32),
            vmem((steps, width, path_cols), F32),
            vmem((width, factors), F32),
            vmem((1, width), F32),
            vmem((1, slices), F32),
            vmem((1, slices), F32),
            vmem((1, slices), F32),
            vmem((1, width), jnp.int32),
            vmem((1, trades_here), F32),
            vmem((1, trades_here), F32),
            vmem((1, trades_here), jnp.int32),
            vmem((1, trades_here), jnp.int32),
            vmem((1, sets), F32),
            vmem((groups, 1, 2 * width), F32),
            vmem((SHARES, slots, width, LANES), BF16),
            vmem((factors, factors), BF16),
            vmem((groups, path_rows, 2 * width), BF16),
            vmem((groups, path_rows, 2 * width), BF16),
            vmem((SHARES, groups + 1, 3, 1, tile), F32),
            vmem((steps, paths, factors), F32),
            vmem((groups, rows, 2 * width + PAD), BF16),
            vmem((SHARES, groups, rows, tile), BF16),
            vmem((rows, sets), F32),
            vmem((rows, sets), BF16),
            vmem((groups, rows, width), F32),
            vmem((groups, paths // 2, 2 * width), BF16),
            dma((13,)),
            dma((8,)),
            dma((8,)),
            dma((2, SHARES)),
        ],
        compiler_params=pltpu.CompilerParams(
            collective_id=0, has_side_effects=True, vmem_limit_bytes=56 * 1024 * 1024
        ),
    )(
        x_start,
        shocks,
        cholesky.T,
        reversion[None, :],
        sabr_alpha[None, :],
        sabr_rho[None, :],
        sabr_nu[None, :],
        factor_slice[None, :],
        notional[None, :],
        strike[None, :],
        trade_set[None, :],
        trade_factor[None, :],
        loss_given[None, :],
    )
    return pl.pallas_call(
        finish_kernel,
        out_shape=(
            jax.ShapeDtypeStruct((width, path_cols), F32),
            jax.ShapeDtypeStruct((3, slices), F32),
        ),
        in_specs=[whole] * 2,
        out_specs=(whole,) * 2,
    )(back, totals)


def solution(mesh):
    return jax.shard_map(
        per_device,
        mesh=mesh,
        in_specs=(
            P("factors", "paths"),
            P(None, "factors", "paths"),
            P(None, "factors"),
            P("factors"),
            P(),
            P(),
            P(),
            P("factors"),
            P("factors"),
            P("factors"),
            P("factors"),
            P("factors"),
            P(),
        ),
        out_specs=(P("factors", "paths"), P()),
        check_vma=False,
    )
```

```python
import functools
import math

import jax
import jax.numpy as jnp
from jax import lax
from jax.experimental import pallas as pl
from jax.experimental.pallas import tpu as pltpu
from jax.sharding import PartitionSpec as P

TIME_STEP = 0.25
ROOT_STEP = 0.5
DISCOUNT_RATE = 0.03
PRECISE = lax.Precision.HIGHEST
MESH = pl.DeviceIdType.MESH
NN = (((1,), (0,)), ((), ()))
NT = (((1,), (1,)), ((), ()))
F32 = jnp.float32
BF16 = jnp.bfloat16
SHARES = 4
PAD = 16
LANES = 128
RUN = 2


def mm(a, b, dims):
    return lax.dot_general(a, b, dims, preferred_element_type=F32)


def split(a):
    high = a.astype(BF16)
    return high, (a - high.astype(F32)).astype(BF16)


def split3(a):
    high, rest = a.astype(BF16), a - a.astype(BF16).astype(F32)
    return (high,) + split(rest)


def one_hot(ids, count, value=None):
    shape = (count, ids.shape[1])
    rows = lax.broadcasted_iota(jnp.int16, shape, 0)
    value = jnp.ones((1, 1), BF16) if value is None else value.astype(BF16)
    hit = rows == jnp.broadcast_to(ids.astype(jnp.int16), shape)
    return jnp.where(hit, jnp.broadcast_to(value, shape), jnp.zeros(shape, BF16))


def wrap(n, size):
    return jnp.where(n >= size, n - size, n)


def pieces_before(g, per_chunk, chunks):
    level = g // per_chunk
    return per_chunk * (chunks * level - level * (level - 1) // 2) + g % per_chunk * (chunks - level)


def fused_kernel(
    x_hbm,
    shocks_hbm,
    lt_hbm,
    reversion_hbm,
    alpha_hbm,
    rho_hbm,
    nu_hbm,
    slice_hbm,
    notional_hbm,
    strike_hbm,
    set_hbm,
    factor_hbm,
    loss_hbm,
    back,
    totals,
    x_ref,
    shocks_ref,
    lt_ref,
    reversion_ref,
    alpha_ref,
    rho_ref,
    nu_ref,
    slice_ref,
    notional_ref,
    strike_ref,
    set_ref,
    factor_ref,
    loss_ref,
    par,
    blocks,
    corr_ref,
    xs_send,
    xs,
    trades,
    states,
    parts,
    squashes,
    exposure,
    weights,
    terms,
    back_send,
    load,
    send_sems,
    recv_sems,
    share_sems,
):
    steps, width, path_cols = shocks_ref.shape
    groups = xs.shape[0]
    factors = corr_ref.shape[0]
    paths = path_cols // groups
    devices = totals.shape[0]
    path_groups = devices // groups
    sets = loss_ref.shape[1]
    slices = alpha_ref.shape[1]
    tile = trades.shape[4]
    pairs = steps // 2
    half = paths // 2
    slots = blocks.shape[1]
    bits = (sets - 1).bit_length()
    chunks = factors // LANES
    per_chunk = LANES // width

    me_f = lax.axis_index("factors")
    me_p = lax.axis_index("paths")
    share = me_p % SHARES
    share_base = me_p - share
    me = me_p * groups + me_f

    pairs_in = [
        (lt_hbm, lt_ref),
        (reversion_hbm, reversion_ref),
        (slice_hbm, slice_ref),
        (x_hbm, x_ref),
        (shocks_hbm, shocks_ref),
        (notional_hbm, notional_ref),
        (strike_hbm, strike_ref),
        (set_hbm, set_ref),
        (factor_hbm, factor_ref),
        (alpha_hbm, alpha_ref),
        (rho_hbm, rho_ref),
        (nu_hbm, nu_ref),
        (loss_hbm, loss_ref),
    ]
    loads = [
        pltpu.make_async_copy(src, dst, load.at[n]) for n, (src, dst) in enumerate(pairs_in)
    ]

    def loaded(*which):
        for n in which:
            loads[n].wait()

    loads[0].start()

    def device_at(d):
        if isinstance(d, tuple):
            return {"paths": wrap(me_p + d[0], path_groups), "factors": wrap(me_f + d[1], groups)}
        return {"factors": wrap(me_f + d, groups)}

    others = [(e, d) for e in range(path_groups) for d in range(groups) if e + d]
    barrier = pltpu.get_barrier_semaphore()
    near = [(e, d) for e, d in others if e == 0 or d == 0]
    for at in near:
        pl.semaphore_signal(barrier, inc=1, device_id=device_at(at), device_id_type=MESH)
    for copy in loads[1:]:
        copy.start()

    def owned(g):
        level = g // per_chunk
        before = pieces_before(g, per_chunk, chunks)
        step = (share - before % SHARES + SHARES) % SHARES
        return level + step, (before + step) // SHARES

    my_chunk, my_slot = owned(me_f)
    my_cols = pl.ds(pl.multiple_of(my_chunk % chunks * LANES, LANES), LANES)
    loaded(0)

    @pl.when(my_chunk < chunks)
    def _():
        blocks[share, my_slot] = lt_ref[:, my_cols].astype(BF16)

    loaded(1, 2)
    par[me_f] = jnp.concatenate([reversion_ref[...], slice_ref[...].astype(F32)], axis=1)
    pl.semaphore_wait(barrier, len(near))

    def start(src, dst, kind, peer):
        pltpu.make_async_remote_copy(
            src_ref=src,
            dst_ref=dst,
            send_sem=send_sems.at[kind],
            recv_sem=recv_sems.at[kind],
            device_id=peer,
            device_id_type=MESH,
        ).start()

    def wait(ref, sem):
        pltpu.make_async_copy(ref, ref, sem).wait()

    away = range(1, groups)
    rest = pl.ds(0, groups - 1)

    @pl.when(my_chunk < chunks)
    def _():
        for d in away:
            start(blocks.at[share, my_slot], blocks.at[share, my_slot], 0, device_at(d))

    for d in away:
        start(par.at[me_f], par.at[me_f], 7, device_at(d))
    loaded(3, 4)
    columns = [jnp.concatenate([x_ref[...], shocks_ref[0]], axis=0).astype(BF16).T]
    for k in range(1, pairs):
        pair = jnp.concatenate([shocks_ref[2 * k - 1], shocks_ref[2 * k]], axis=0)
        columns.append(pair.astype(BF16).T)
    final = shocks_ref[steps - 1].astype(BF16).T
    for g in range(groups):
        top = g * paths
        for k in range(pairs):
            xs_send[g, k * paths : (k + 1) * paths] = columns[k][top : top + paths]
        xs_send[g, pairs * paths :] = jnp.concatenate(
            [final[top : top + half], final[top + half : top + paths]], axis=1
        )
    xs[me_f] = xs_send[me_f]
    for d in away:
        start(xs_send.at[wrap(me_f + d, groups)], xs.at[me_f], 2, device_at(d))

    loaded(5, 6, 7, 8)
    for n in range(SHARES):
        cols = slice(n * tile, (n + 1) * tile)
        code = set_ref[:, cols] + ((factor_ref[:, cols] - me_f * width) << bits)
        trades[n, groups, 0] = notional_ref[:, cols]
        trades[n, groups, 1] = strike_ref[:, cols]
        trades[n, groups, 2] = code.astype(F32)
    trades[share, me_f] = trades[share, groups]
    for d in away:
        start(trades.at[share, me_f], trades.at[share, me_f], 1, device_at(d))

    @pl.when(my_chunk < chunks)
    def _():
        wait(blocks.at[share, pl.ds(0, slots - 1)], recv_sems.at[0])

    @pl.when(my_chunk >= chunks)
    def _():
        wait(blocks.at[share], recv_sems.at[0])

    def paired(d):
        if d == 2:
            return wrap(share + 2, SHARES)
        return share + 1 - 2 * (share % 2) if d == 1 else SHARES - 1 - share

    def start_share(ref, kind):
        for d in (2, 3, 1):
            peer = {"paths": share_base + paired(d)}
            pltpu.make_async_remote_copy(
                src_ref=ref,
                dst_ref=ref,
                send_sem=send_sems.at[kind],
                recv_sem=share_sems.at[kind - 3, d],
                device_id=peer,
                device_id_type=MESH,
            ).start()

    start_share(blocks.at[share], 3)
    loaded(9, 10, 11, 12)
    wait(par.at[rest], recv_sems.at[7])
    all_par = [par[g] for g in range(groups)]
    damping = 1.0 - jnp.concatenate([p[:, :width] for p in all_par], axis=1) * TIME_STEP
    slice_ids = jnp.concatenate([p[:, width:] for p in all_par], axis=1)
    slice_rows = lax.broadcasted_iota(jnp.int32, (slices, factors), 0).astype(F32)
    slice_table = jnp.where(slice_rows == slice_ids, 1.0, 0.0).astype(BF16)
    smile = jnp.concatenate(
        [alpha_ref[...], rho_ref[...], nu_ref[...], jnp.zeros((5, slices), F32)], axis=0
    )
    smile = mm(jnp.concatenate(split3(smile), axis=0), slice_table, NN)
    smile = smile[0:8] + (smile[8:16] + smile[16:24])
    alpha, rho, nu = smile[0:1, :], smile[1:2, :], smile[2:3, :]
    curve2 = 2.0 - 3.0 * rho * rho
    curve = curve2 * nu * nu / 24.0
    tilt = 0.5 * rho * nu

    for d in range(1, SHARES):
        wait(blocks.at[paired(d)], share_sems.at[0, d])
    empty = jnp.zeros((width, LANES), BF16)
    for g in range(groups):
        first = pieces_before(g, per_chunk, chunks)
        level = g // per_chunk
        for c in range(chunks):
            n = first + c - level
            corr_ref[g * width : (g + 1) * width, c * LANES : (c + 1) * LANES] = (
                empty if c < level else blocks[n % SHARES, n // SHARES]
            )
    wait(xs.at[rest], recv_sems.at[2])
    low_rows = pairs * paths + half
    both = [xs[g].astype(F32) for g in range(groups)]
    lefts = jnp.concatenate([b[:, :width] for b in both], axis=1)
    rights = jnp.concatenate([b[:, width:] for b in both], axis=1)
    state = lefts[:paths]
    shocks = [rights[:paths]]
    for k in range(1, pairs):
        shocks.extend([lefts[k * paths : (k + 1) * paths], rights[k * paths : (k + 1) * paths]])
    shocks.append(
        jnp.concatenate([lefts[pairs * paths : low_rows], rights[pairs * paths : low_rows]], axis=0)
    )
    ones = jnp.ones((paths, PAD), BF16)
    for k in range(steps):
        states[k] = state
        u = jnp.tanh(state)
        source = alpha * (1.0 + tilt * u + curve * u * u) * shocks[k]
        state = damping * state + ROOT_STEP * mm(source.astype(BF16), corr_ref[...], NN)
        high, low = split(state)
        for b in range(groups):
            cols = slice(b * width, (b + 1) * width)
            parts[b, k * paths : (k + 1) * paths, :] = jnp.concatenate(
                [high[:, cols], low[:, cols], ones], axis=1
            )


    def trade_rows(s, b):
        code = trades[s, b, 2].astype(jnp.int32)
        return trades[s, b, 0], trades[s, b, 1], code & ((1 << bits) - 1), code >> bits

    def forward(s, slot, b=None, first=False):
        b = slot if b is None else b
        notional, strike, in_set, factor = trade_rows(s, slot)
        table = one_hot(factor, width)
        high, low = split(-strike)
        tail = jnp.concatenate([high, low, jnp.zeros((PAD - 2, tile), BF16)], axis=0)
        money = mm(parts[b], jnp.concatenate([table, table, tail], axis=0), NN)
        squash = jnp.tanh(money).astype(BF16)
        squashes[s, b] = squash
        got = mm(squash, one_hot(in_set, sets, notional), NT)
        exposure[...] = got if first else exposure[...] + got

    every = pl.ds(0, groups)
    wait(trades.at[share, rest], recv_sems.at[1])
    start_share(trades.at[share, every], 4)
    for n in range(SHARES):
        forward(n, groups, me_f, n == 0)
    for n in away:
        forward(share, wrap(me_f + n, groups))
    wait(trades.at[paired(1), every], share_sems.at[1, 1])
    for n in away:
        forward(paired(1), wrap(me_f + n, groups))
    for d in (2, 3):
        wait(trades.at[paired(d), every], share_sems.at[1, d])
    for n in away:
        for d in (2, 3):
            forward(paired(d), wrap(me_f + n, groups))

    for k in range(steps):
        at = slice(k * paths, (k + 1) * paths)
        scale = math.exp(-DISCOUNT_RATE * TIME_STEP * (k + 1)) * loss_ref[...]
        weights[at, :] = (scale * jax.nn.sigmoid(exposure[at, :])).astype(BF16)

    def backward(s, b):
        notional, strike, in_set, factor = trade_rows(s, b)
        pulled = mm(weights[...], one_hot(in_set, sets), NN)
        squash = squashes[s, b].astype(F32)
        pulled = (pulled * (notional * (1.0 - squash * squash))).astype(BF16)
        return mm(pulled, one_hot(factor, width), NT)

    for first in range(0, groups, RUN):

        @pl.when(me_f >= 0)
        def _():
            for b in range(first, first + RUN):
                for s in range(SHARES):
                    got = backward(s, b)
                    terms[b] = got if s == 0 else terms[b] + got


    adjoint = jnp.zeros((paths, factors), F32)
    sums = [jnp.zeros((1, factors), F32) for _ in range(3)]
    for k in reversed(range(steps)):
        adjoint = adjoint + jnp.concatenate(
            [terms[b, k * paths : (k + 1) * paths, :] for b in range(groups)], axis=1
        )
        u = jnp.tanh(states[k])
        vbar = mm((ROOT_STEP * adjoint).astype(BF16), corr_ref[...], NT) * shocks[k]
        for at, slope in enumerate(
            (
                1.0 + tilt * u + curve * u * u,
                alpha * (0.5 * nu * u - 0.25 * rho * nu * nu * u * u),
                alpha * (0.5 * rho * u + curve2 * nu * u * u / 12.0),
            )
        ):
            sums[at] = sums[at] + jnp.sum(vbar * slope, axis=0, keepdims=True)
        adjoint = damping * adjoint + vbar * (alpha * (tilt + 2.0 * curve * u)) * (1.0 - u * u)

    for g in range(groups):
        cols = slice(g * width, (g + 1) * width)
        back_send[g] = jnp.concatenate([adjoint[:half, cols], adjoint[half:, cols]], axis=1).astype(BF16)

    for d in away:
        start(back_send.at[wrap(me_f + d, groups)], back.at[me_f], 5, device_at(d))
    back[me_f] = back_send[me_f]
    stacked = jnp.concatenate(sums + [jnp.zeros((5, factors), F32)], axis=0)
    thirds = mm(jnp.concatenate(split3(stacked), axis=0), slice_table, NT)
    rows = thirds[0:8] + (thirds[8:16] + thirds[16:24])
    totals[me] = jnp.concatenate([rows[n : n + 1] for n in range(4)], axis=1)
    for at in others:
        start(totals.at[me], totals.at[me], 6, device_at(at))

    @pl.when(my_chunk < chunks)
    def _():
        for _ in away:
            wait(blocks.at[share, my_slot], send_sems.at[0])

    wait(trades.at[share, rest], send_sems.at[1])
    wait(xs.at[rest], send_sems.at[2])
    wait(par.at[rest], send_sems.at[7])
    for d in range(1, SHARES):
        wait(blocks.at[share], send_sems.at[3])
        wait(trades.at[share, every], send_sems.at[4])
    wait(back.at[rest], send_sems.at[5])
    wait(totals.at[pl.ds(0, len(others))], send_sems.at[6])
    wait(back.at[rest], recv_sems.at[5])
    wait(totals.at[pl.ds(0, len(others))], recv_sems.at[6])


def finish_kernel(back_ref, totals_ref, a_ref, g_ref):
    groups = back_ref.shape[0]
    width, path_cols = a_ref.shape
    slices = g_ref.shape[1]
    pieces = []
    for g in range(groups):
        piece = back_ref[g].astype(F32)
        pieces.extend([piece[:, :width], piece[:, width:]])
    a_ref[...] = jnp.concatenate(pieces, axis=0).T
    path_groups = totals_ref.shape[0] // groups
    total = jnp.sum(totals_ref[...], axis=0) / (path_cols * path_groups)
    g_ref[...] = jnp.concatenate([total[:, n * slices : (n + 1) * slices] for n in range(3)], axis=0)


def per_device(
    x_start,
    shocks,
    cholesky,
    reversion,
    sabr_alpha,
    sabr_rho,
    sabr_nu,
    factor_slice,
    notional,
    strike,
    trade_set,
    trade_factor,
    loss_given,
):
    width, path_cols = x_start.shape
    steps, factors = shocks.shape[0], cholesky.shape[0]
    groups = lax.axis_size("factors")
    path_groups = lax.axis_size("paths")
    devices = groups * path_groups
    paths = path_cols // groups
    trades_here = notional.shape[0]
    tile = trades_here // SHARES
    rows, sets, slices = steps * paths, loss_given.shape[0], sabr_alpha.shape[0]
    fold = LANES // width
    pairs = steps // 2
    path_rows = pairs * paths + paths // 2
    slots = pieces_before(groups, fold, factors // LANES) // SHARES
    vmem, dma = pltpu.VMEM, pltpu.SemaphoreType.DMA
    whole = pl.BlockSpec(memory_space=pltpu.VMEM)
    back, totals = pl.pallas_call(
        fused_kernel,
        out_shape=(
            jax.ShapeDtypeStruct((groups, paths // 2, 2 * width), BF16),
            jax.ShapeDtypeStruct((devices, 1, 4 * slices), F32),
        ),
        in_specs=[pl.BlockSpec(memory_space=pl.ANY)] * 13,
        out_specs=(whole,) * 2,
        scratch_shapes=[
            vmem((width, path_cols), F32),
            vmem((steps, width, path_cols), F32),
            vmem((width, factors), F32),
            vmem((1, width), F32),
            vmem((1, slices), F32),
            vmem((1, slices), F32),
            vmem((1, slices), F32),
            vmem((1, width), jnp.int32),
            vmem((1, trades_here), F32),
            vmem((1, trades_here), F32),
            vmem((1, trades_here), jnp.int32),
            vmem((1, trades_here), jnp.int32),
            vmem((1, sets), F32),
            vmem((groups, 1, 2 * width), F32),
            vmem((SHARES, slots, width, LANES), BF16),
            vmem((factors, factors), BF16),
            vmem((groups, path_rows, 2 * width), BF16),
            vmem((groups, path_rows, 2 * width), BF16),
            vmem((SHARES, groups + 1, 3, 1, tile), F32),
            vmem((steps, paths, factors), F32),
            vmem((groups, rows, 2 * width + PAD), BF16),
            vmem((SHARES, groups, rows, tile), BF16),
            vmem((rows, sets), F32),
            vmem((rows, sets), BF16),
            vmem((groups, rows, width), F32),
            vmem((groups, paths // 2, 2 * width), BF16),
            dma((13,)),
            dma((8,)),
            dma((8,)),
            dma((2, SHARES)),
        ],
        compiler_params=pltpu.CompilerParams(
            collective_id=0, has_side_effects=True, vmem_limit_bytes=56 * 1024 * 1024
        ),
    )(
        x_start,
        shocks,
        cholesky.T,
        reversion[None, :],
        sabr_alpha[None, :],
        sabr_rho[None, :],
        sabr_nu[None, :],
        factor_slice[None, :],
        notional[None, :],
        strike[None, :],
        trade_set[None, :],
        trade_factor[None, :],
        loss_given[None, :],
    )
    return pl.pallas_call(
        finish_kernel,
        out_shape=(
            jax.ShapeDtypeStruct((width, path_cols), F32),
            jax.ShapeDtypeStruct((3, slices), F32),
        ),
        in_specs=[whole] * 2,
        out_specs=(whole,) * 2,
    )(back, totals)


def solution(mesh):
    return jax.shard_map(
        per_device,
        mesh=mesh,
        in_specs=(
            P("factors", "paths"),
            P(None, "factors", "paths"),
            P(None, "factors"),
            P("factors"),
            P(),
            P(),
            P(),
            P("factors"),
            P("factors"),
            P("factors"),
            P("factors"),
            P("factors"),
            P(),
        ),
        out_specs=(P("factors", "paths"), P()),
        check_vma=False,
    )
```
